128 devices in a mesh: px: 8 (over x, core), py: 16 (over y, z).
Axes of the slice: x: 4, y: 4, z: 4, core: 2. Of those that a mesh axis runs over, the one named last changes fastest.
Arguments:
- fine_state: float32 [5, 216, 65536], P(None, None, ('px', 'py')), may hold values from -0.3 to 3.5, as said below
- fine_register: float32 [5, 216, 65536], P(None, None, ('px', 'py')), may hold values from -0.4 to 0.4
- coarse_state: float32 [5, 216, 32768], P(None, None, ('px', 'py')), may hold values from -0.3 to 3.5, as said below
- coarse_register: float32 [5, 216, 32768], P(None, None, ('px', 'py')), may hold values from -0.4 to 0.4
- coarse_owner: int32 [128, 128], P('px', 'py'), may hold values from 0 to 32767, as said below
- coarse_count: int32 [128], P(('px', 'py')), may hold values from 0 to 256, as said below
Outputs:
- fine_out: float32 [5, 216, 65536], P(None, None, ('px', 'py'))
- fine_register_out: float32 [5, 216, 65536], P(None, None, ('px', 'py'))
- coarse_out: float32 [5, 216, 32768], P(None, None, ('px', 'py'))
- coarse_register_out: float32 [5, 216, 32768], P(None, None, ('px', 'py'))
The draws below stay inside these ranges and needn't reach their ends.
Inputs may be any that keep to these rules, and one draw needn't show every extreme that they name: `fine_state`: component 0 lies in 1.0 to 1.5, components 1 to 3 in -0.3 to 0.3, component 4 in 2.5 to 3.5. `coarse_state`: component 0 lies in 1.0 to 1.5, components 1 to 3 in -0.3 to 0.3, component 4 in 2.5 to 3.5. `coarse_owner`: each entry is owner * 256 + slot, where the owner device has the same px index as the device holding the entry; every live slot of every device is named exactly once; each device's entries name at most 16 slots of one owner, and some reach it. The live slots of device d are its slots 0 to coarse_count[d] - 1; some device has 256.
All inputs are finite; a program needn't handle non-finite values.
Results may differ from the reference program's by a relative error of at most 0.0001.
Values sent between devices are 32-bit elements; how exact they have to be, the bound alone decides.
A program may use at most 192 MiB of HBM per device.

```python
import math
import jax
import jax.numpy as jnp
import numpy as np
from jax import lax

NP = 6
NODES = 216
EX = 32
EY = 16
EZ = 1
ELEMS = 65536
CE = 256
COARSE = 32768
NCX = 128
NCY = 128
N_PX = 8
N_PY = 16
DEVICES = 128


def owner_plan(key):
    peers = N_PY
    cells = EX // 2 * (EY // 2)
    mean = cells // peers
    quarter = peers // 4

    def row_plan(row_key, row):
        keys = jax.random.split(row_key, 4)
        order = jax.random.permutation(keys[0], peers)
        rank = jnp.zeros((peers,), jnp.int32).at[order].set(jnp.arange(peers, dtype=jnp.int32))
        load = jnp.where(rank < quarter, 2 * mean, jnp.where(rank < 3 * quarter, mean, 0)).astype(jnp.int32)
        loads = jnp.broadcast_to(load[None, :], (peers, peers))
        first = jax.random.randint(keys[1], (), 0, peers)
        second = (first + 1 + jax.random.randint(keys[2], (), 0, peers - 1)) % peers
        change = mean // 2
        owner_one = order[quarter]
        owner_two = order[quarter + 1]
        delta = jnp.zeros((peers, peers), jnp.int32)
        delta = delta.at[first, owner_one].add(change).at[first, owner_two].add(-change)
        delta = delta.at[second, owner_one].add(-change).at[second, owner_two].add(change)
        loads = loads + delta
        ending = jnp.cumsum(loads, axis=1)
        starting = ending - loads
        position = jnp.arange(cells, dtype=jnp.int32)
        owner_of = jnp.sum((position[None, :, None] >= ending[:, None, :]).astype(jnp.int32), axis=2)
        within = position[None, :] - jnp.take_along_axis(starting, owner_of, axis=1)
        earlier = jnp.cumsum(loads, axis=0) - loads
        slot = jnp.take_along_axis(earlier, owner_of, axis=1) + within
        global_id = (row * peers + owner_of) * CE + slot
        shuffles = jax.vmap(lambda sub: jax.random.permutation(sub, cells))(jax.random.split(keys[3], peers))
        senders = jnp.arange(peers, dtype=jnp.int32)[:, None]
        placed = jnp.zeros((peers, cells), jnp.int32).at[senders, shuffles].set(global_id)
        return (placed.reshape(peers, EX // 2, EY // 2), jnp.sum(loads, axis=0))
    row_keys = jax.random.split(key, N_PX)
    placed, counts = jax.vmap(row_plan)(row_keys, jnp.arange(N_PX, dtype=jnp.int32))
    placed = placed.transpose(0, 2, 1, 3).reshape(N_PX * (EX // 2), N_PY * (EY // 2))
    return (placed.astype(jnp.int32), counts.reshape(N_PX * N_PY).astype(jnp.int32))


def draw_coarse_owner(key, part):
    return owner_plan(jax.random.fold_in(key, 7))[0]


def draw_coarse_count(key, part):
    return owner_plan(jax.random.fold_in(key, 7))[1]


def draw_fine_state(key, part):
    lower = jnp.array([1.0, -0.3, -0.3, -0.3, 2.5], jnp.float32).reshape(5, 1, 1)
    upper = jnp.array([1.5, 0.3, 0.3, 0.3, 3.5], jnp.float32).reshape(5, 1, 1)
    unit = jax.random.uniform(jax.random.fold_in(key, 11), (5, NODES, ELEMS), jnp.float32)
    return lower + (upper - lower) * unit


def draw_coarse_state(key, part):
    lower = jnp.array([1.0, -0.3, -0.3, -0.3, 2.5], jnp.float32).reshape(5, 1, 1)
    upper = jnp.array([1.5, 0.3, 0.3, 0.3, 3.5], jnp.float32).reshape(5, 1, 1)
    unit = jax.random.uniform(jax.random.fold_in(key, 13), (5, NODES, COARSE), jnp.float32)
    return lower + (upper - lower) * unit


def levels(stream_key, dims, pieces, least, top_value):
    def one(dim, blocks):
        heights = jax.random.uniform(jax.random.fold_in(jax.random.fold_in(stream_key, 6), dim), (blocks,), jnp.float32, least / len(pieces), top_value / len(pieces))
        return jnp.repeat(jnp.exp(heights), dims[dim] // blocks).reshape((-1,) + (1,) * (len(dims) - dim - 1))

    loudness = one(*pieces[0])
    for cut in pieces[1:]:
        loudness = loudness * one(*cut)
    return loudness


def bell_draw(rng, dims, width, bound, shards=(), held_as=jnp.bfloat16):
    entries = jax.random.normal(rng, dims, jnp.float32) * width
    if len(shards) > 0:
        entries = levels(rng, dims, shards, -0.22, 0.18) * entries
    return jnp.clip(entries, min=-bound, max=bound).astype(held_as)


def setup_inputs(seed: int = 0) -> dict:
    arg_keys = jax.random.split(jax.random.key(seed), 7)
    return {
        "fine_state": draw_fine_state(jax.random.fold_in(arg_keys[6], 71), 0),
        "fine_register": bell_draw(arg_keys[1], (5, NODES, ELEMS), 0.1, 0.4, ((2, 128),), jnp.float32),
        "coarse_state": draw_coarse_state(jax.random.fold_in(arg_keys[6], 71), 0),
        "coarse_register": bell_draw(arg_keys[3], (5, NODES, COARSE), 0.1, 0.4, ((2, 128),), jnp.float32),
        "coarse_owner": draw_coarse_owner(jax.random.fold_in(arg_keys[6], 71), 0),
        "coarse_count": draw_coarse_count(jax.random.fold_in(arg_keys[6], 71), 0),
    }


time_step = 0.01
section_coefs = ((-0.4178904745, 0.3792103129), (-1.192151694643, 0.8229550293869))

def legendre_columns(nodes, points):
    columns = [np.ones(points), nodes]
    for degree in range(2, points):
        columns.append(((2 * degree - 1) * nodes * columns[-1] - (degree - 1) * columns[-2]) / degree)
    return columns

def node_tables(points):
    order = points - 1
    nodes = np.array([-math.cos(math.pi * index / order) for index in range(points)])
    for sweep in range(60):
        columns = legendre_columns(nodes, points)
        nodes = nodes - (nodes * columns[order] - columns[order - 1]) / (points * columns[order])
    legendre = legendre_columns(nodes, points)[order]
    weights = 2.0 / (order * points * legendre ** 2)
    same = np.arange(points)[:, None] == np.arange(points)[None, :]
    spread = nodes[:, None] - nodes[None, :] + np.where(same, 1.0, 0.0)
    barycentric = 1.0 / np.prod(spread, axis=1)
    derivative = np.where(same, 0.0, barycentric[None, :] / barycentric[:, None] / spread)
    derivative = derivative - np.where(same, np.sum(derivative, axis=1)[:, None], 0.0)
    halves = []
    for side in (-1.0, 1.0):
        target = 0.5 * (nodes + side)
        table = np.ones((points, points))
        for column in range(points):
            for other in range(points):
                if other != column:
                    table[:, column] *= (target - nodes[other]) / (nodes[column] - nodes[other])
        halves.append(table)
    to_fine = np.stack(halves)
    to_coarse = 0.5 * to_fine.transpose(0, 2, 1) * weights[None, None, :] / weights[None, :, None]
    return (jnp.asarray(derivative, dtype=jnp.float32), jnp.asarray(to_fine, dtype=jnp.float32), jnp.asarray(to_coarse, dtype=jnp.float32), float(1.0 / weights[0]))

def flux_speed(state, direction):
    inverse = 1.0 / state[0]
    velocity = state[1 + direction] * inverse
    pressure = 0.4 * (state[4] - 0.5 * (state[1] * state[1] + state[2] * state[2] + state[3] * state[3]) * inverse)
    parts = [state[1 + direction], state[1] * velocity, state[2] * velocity, state[3] * velocity, (state[4] + pressure) * velocity]
    parts[1 + direction] = parts[1 + direction] + pressure
    speed = jnp.abs(velocity) + jnp.sqrt(1.4 * pressure * inverse)
    return (jnp.stack(parts), speed)

def interface(left_state, right_state, direction):
    left_flux, left_speed = flux_speed(left_state, direction)
    right_flux, right_speed = flux_speed(right_state, direction)
    return 0.5 * (left_flux + right_flux) - 0.5 * jnp.maximum(left_speed, right_speed) * (right_state - left_state)

def volume(state, derivative, factor):
    first = flux_speed(state, 0)[0]
    second = flux_speed(state, 1)[0]
    third = flux_speed(state, 2)[0]
    total = jnp.einsum('ai,vijk...->vajk...', derivative, first, precision=lax.Precision.HIGHEST)
    total = total + jnp.einsum('aj,vijk...->viak...', derivative, second, precision=lax.Precision.HIGHEST)
    total = total + jnp.einsum('ak,vijk...->vija...', derivative, third, precision=lax.Precision.HIGHEST)
    return -factor * total

def along_grid(trace):
    moved = jnp.moveaxis(trace, 4, 5)
    return moved.reshape(5, NP, NP, N_PX * EX, N_PY * EY, EZ)

def to_blocks(trace):
    return jnp.moveaxis(trace.reshape(5, NP, NP, N_PX, EX, N_PY, EY, EZ), 5, 4)

def residuals(fine, coarse, slot_ids, tables):
    derivative, to_fine, to_coarse, lifting = tables
    points = NP
    block = EX * EY * EZ
    scale = 2.0 * lifting
    blocks = jnp.moveaxis(fine.reshape(5, NODES, DEVICES, block), 2, 0)
    vol = lax.map(lambda piece: volume(piece.reshape(5, points, points, points, block), derivative, 2.0), blocks)
    result = jnp.moveaxis(vol, 0, 4).reshape(5, points, points, points, N_PX, N_PY, EX, EY, EZ)
    grid = fine.reshape(5, points, points, points, N_PX, N_PY, EX, EY, EZ)
    for direction in range(2):
        if direction == 0:
            minus_face, plus_face = (along_grid(grid[:, 0]), along_grid(grid[:, points - 1]))
        else:
            minus_face, plus_face = (along_grid(grid[:, :, 0]), along_grid(grid[:, :, points - 1]))
        low_flux = interface(jnp.roll(plus_face, 1, axis=3 + direction), minus_face, direction)
        high_flux = jnp.roll(low_flux, -1, axis=3 + direction)
        low_term = to_blocks(scale * (low_flux - flux_speed(minus_face, direction)[0]))
        high_term = to_blocks(scale * (flux_speed(plus_face, direction)[0] - high_flux))
        if direction == 0:
            result = result.at[:, 0].add(low_term).at[:, points - 1].add(high_term)
        else:
            result = result.at[:, :, 0].add(low_term).at[:, :, points - 1].add(high_term)
    minus_face = along_grid(grid[:, :, :, 0])
    plus_face = along_grid(grid[:, :, :, points - 1])
    ground = minus_face[..., 0:1]
    mirror = jnp.concatenate([ground[:3], -ground[3:4], ground[4:]], 0)
    below = jnp.concatenate([interface(mirror, ground, 2), interface(plus_face[..., :-1], minus_face[..., 1:], 2)], -1)
    upper = plus_face[..., EZ - 1]
    cell_count = NCX * NCY
    fine_cells = upper.reshape(5, points, points, NCX, 2, NCY, 2).transpose(0, 1, 2, 4, 6, 3, 5)
    fine_cells = fine_cells.reshape(5, points, points, 2, 2, cell_count)
    coarse_grid = coarse.reshape(5, points, points, points, COARSE)
    bottom = coarse_grid[:, :, :, 0]
    partner = jnp.take(bottom, slot_ids, axis=3)
    lifted = jnp.einsum('api,bqj,vijc->vpqabc', to_fine, to_fine, partner, precision=lax.Precision.HIGHEST)
    mortar = interface(fine_cells, lifted, 2)
    top_flux = mortar.reshape(5, points, points, 2, 2, NCX, NCY).transpose(0, 1, 2, 5, 3, 6, 4)
    top_flux = top_flux.reshape(5, points, points, N_PX * EX, N_PY * EY)
    above = jnp.concatenate([below[..., 1:], top_flux[..., None]], -1)
    low_term = to_blocks(scale * (below - flux_speed(minus_face, 2)[0]))
    high_term = to_blocks(scale * (flux_speed(plus_face, 2)[0] - above))
    result = result.at[:, :, :, 0].add(low_term).at[:, :, :, points - 1].add(high_term)
    projected = jnp.einsum('aip,bjq,vpqabc->vijc', to_coarse, to_coarse, mortar, precision=lax.Precision.HIGHEST)
    face = jnp.zeros((5, points, points, COARSE), jnp.float32).at[:, :, :, slot_ids].set(projected)
    coarse_result = volume(coarse_grid, derivative, 1.0)
    coarse_result = coarse_result.at[:, :, :, 0].add(lifting * (face - flux_speed(bottom, 2)[0]))
    return (result.reshape(5, NODES, ELEMS), coarse_result.reshape(5, NODES, COARSE))

def reference(fine_state, fine_register, coarse_state, coarse_register, coarse_owner, coarse_count):
    tables = node_tables(NP)
    slot_ids = coarse_owner.reshape(NCX * NCY)
    live = jnp.arange(COARSE, dtype=jnp.int32) % CE < jnp.repeat(coarse_count, CE, total_repeat_length=COARSE)
    state, register = (fine_state, fine_register)
    coarse, coarse_reg = (coarse_state, coarse_register)
    for decay_coef, step_coef in section_coefs:
        fine_rate, coarse_rate = residuals(state, coarse, slot_ids, tables)
        register = decay_coef * register + time_step * fine_rate
        state = state + step_coef * register
        new_reg = jnp.where(live, decay_coef * coarse_reg + time_step * coarse_rate, coarse_reg)
        coarse = jnp.where(live, coarse + step_coef * new_reg, coarse)
        coarse_reg = new_reg
    return (state, register, coarse, coarse_reg)
```

```python
import functools
import math

import jax
import jax.numpy as jnp
import numpy as np
from jax import lax
from jax.experimental import pallas as pl
from jax.experimental.pallas import tpu as pltpu
from jax.sharding import PartitionSpec as P

NP = 6
NODES = 216
ROWS = 224
EX = 32
EY = 16
CE = 256
SLOTS = 256
KH = 3 * ROWS

time_step = 0.01
section_coefs = ((-0.4178904745, 0.3792103129), (-1.192151694643, 0.8229550293869))
MESH = pl.DeviceIdType.MESH
F32 = jnp.float32
BF16 = jnp.bfloat16


def legendre_columns(nodes, points):
    columns = [np.ones(points), nodes]
    for degree in range(2, points):
        columns.append(
            ((2 * degree - 1) * nodes * columns[-1] - (degree - 1) * columns[-2]) / degree
        )
    return columns


def node_tables(points):
    order = points - 1
    nodes = np.array([-math.cos(math.pi * index / order) for index in range(points)])
    for sweep in range(60):
        columns = legendre_columns(nodes, points)
        nodes = nodes - (nodes * columns[order] - columns[order - 1]) / (points * columns[order])
    legendre = legendre_columns(nodes, points)[order]
    weights = 2.0 / (order * points * legendre**2)
    same = np.arange(points)[:, None] == np.arange(points)[None, :]
    spread = nodes[:, None] - nodes[None, :] + np.where(same, 1.0, 0.0)
    barycentric = 1.0 / np.prod(spread, axis=1)
    derivative = np.where(same, 0.0, barycentric[None, :] / barycentric[:, None] / spread)
    derivative = derivative - np.where(same, np.sum(derivative, axis=1)[:, None], 0.0)
    halves = []
    for side in (-1.0, 1.0):
        target = 0.5 * (nodes + side)
        table = np.ones((points, points))
        for column in range(points):
            for other in range(points):
                if other != column:
                    table[:, column] *= (target - nodes[other]) / (nodes[column] - nodes[other])
        halves.append(table)
    to_fine = np.stack(halves)
    to_coarse = 0.5 * to_fine.transpose(0, 2, 1) * weights[None, None, :] / weights[None, :, None]
    f = np.float32
    return derivative.astype(f), to_fine.astype(f), to_coarse.astype(f), float(1.0 / weights[0])


def halves_of(table):
    high = np.asarray(table, np.float32).astype(BF16)
    low = (np.asarray(table, np.float32) - high.astype(np.float32)).astype(BF16)
    return high, low


def make_tables():
    derivative, to_fine, to_coarse, lifting = node_tables(NP)
    eye = np.eye(NP, dtype=np.float32)
    mats = (
        np.kron(np.kron(derivative, eye), eye),
        np.kron(np.kron(eye, derivative), eye),
        np.kron(np.kron(eye, eye), derivative),
    )
    wide = np.zeros((ROWS, KH), np.float32)
    for d in range(3):
        wide[:NODES, d * ROWS : d * ROWS + NODES] = mats[d]
    high, low = halves_of(wide)
    dh = np.concatenate([high, high], axis=1)
    stacks = []
    for table in (to_fine, to_coarse):
        full = np.zeros((160, 48), np.float32)
        for a in range(2):
            for b in range(2):
                r = (2 * a + b) * 40
                full[r : r + 36, :36] = np.kron(table[a], table[b])
        th, tl = halves_of(full)
        stacks.append(np.concatenate([th, th, tl], axis=1))
    return dh, low, stacks[0], stacks[1], lifting


def split(x):
    high = x.astype(BF16)
    low = (x - high.astype(F32)).astype(BF16)
    return high, low


def dot_nn(a, b):
    return lax.dot_general(a, b, (((1,), (0,)), ((), ())), preferred_element_type=F32)


def dot_nt(a, b):
    return lax.dot_general(a, b, (((1,), (1,)), ((), ())), preferred_element_type=F32)


def pressure_of(q, inverse):
    return 0.4 * (q[4] - 0.5 * (q[1] * q[1] + q[2] * q[2] + q[3] * q[3]) * inverse)


def flux(q, d):
    inverse = 1.0 / q[0]
    velocity = q[1 + d] * inverse
    pressure = pressure_of(q, inverse)
    parts = [q[1 + d], q[1] * velocity, q[2] * velocity, q[3] * velocity, (q[4] + pressure) * velocity]
    parts[1 + d] = parts[1 + d] + pressure
    return parts, velocity, pressure, inverse


def flux_speed(q, d):
    parts, velocity, pressure, inverse = flux(q, d)
    return parts, jnp.abs(velocity) + jnp.sqrt(1.4 * pressure * inverse)


def blend(left, left_flux, left_speed, right, right_flux, right_speed):
    fastest = 0.5 * jnp.maximum(left_speed, right_speed)
    return [
        0.5 * (lf + rf) - fastest * (r - l)
        for l, lf, r, rf in zip(left, left_flux, right, right_flux)
    ]


def lanes_of(shape):
    return lax.broadcasted_iota(jnp.int32, shape, len(shape) - 1)


def rows_of(shape):
    return lax.broadcasted_iota(jnp.int32, shape, len(shape) - 2)


def kernel(
    shape, lifting,
    fs, fr, cs, cr, own, cnt, dh, dl, pst, qst,
    ofs, ofr, ocs, ocr,
    Q, G, R, FB, BB, S, W, SEL, MS, PM, TOPC,
    req, wanted, rep, inc, fout, fin, hx, hyo, hy,
    in_sem, out_sem, req_s, req_r, rep_s, rep_r, f_s, f_r, h_s, h_r,
):
    npx, npy = shape
    most = SLOTS // npy
    px = lax.axis_index("px")
    py = lax.axis_index("py")
    up = [(px, lax.rem(py + d, npy)) for d in range(npy)]
    down = [(px, lax.rem(py + npy - d, npy)) for d in range(npy)]
    x_right, x_left = (lax.rem(px + 1, npx), py), (lax.rem(px + npx - 1, npx), py)
    y_right, y_left = up[1], down[1]
    dt = time_step
    lift = dt * lifting
    lift2 = 2.0 * lift

    def remote(src, dst, ss, rs, dev):
        return pltpu.make_async_remote_copy(
            src_ref=src, dst_ref=dst, send_sem=ss, recv_sem=rs, device_id=dev, device_id_type=MESH
        )

    barrier = pltpu.get_barrier_semaphore()
    for d in range(1, npy):
        pl.semaphore_signal(barrier, inc=1, device_id=up[d], device_id_type=MESH)
    pl.semaphore_signal(barrier, inc=1, device_id=x_right, device_id_type=MESH)
    pl.semaphore_signal(barrier, inc=1, device_id=x_left, device_id_type=MESH)

    loads = []
    for t in range(6):
        src = fs if t < 4 else cs
        lane = 128 * (t if t < 4 else t - 4)
        loads.append(
            pltpu.make_async_copy(src.at[:, :, pl.ds(lane, 128)], Q.at[t, :, pl.ds(0, NODES)], in_sem.at[t])
        )
    for t in range(6):
        src = fr if t < 4 else cr
        lane = 128 * (t if t < 4 else t - 4)
        loads.append(
            pltpu.make_async_copy(src.at[:, :, pl.ds(lane, 128)], G.at[t], in_sem.at[6 + t])
        )
    for copy in loads:
        copy.start()

    for t in range(6):
        for v in range(5):
            Q[t, v, pl.ds(NODES, ROWS - NODES), :] = jnp.full(
                (ROWS - NODES, 128), (1.0, 0.0, 0.0, 0.0, 2.5)[v], F32
            )
    for t in range(2):
        BB[t, pl.ds(180, 4), :] = jnp.zeros((4, 128), F32)
        BB[t, pl.ds(364, 20), :] = jnp.zeros((20, 128), F32)
    for t in range(4):
        PM[t, pl.ds(180, 76), :] = jnp.zeros((76, 128), F32)
        for v in range(5):
            MS[t, v, pl.ds(36, 12), :] = jnp.zeros((12, 128), F32)

    owner = own[...]
    spread = (lanes_of((8, 128)) % 8 == rows_of((8, 128))).astype(BF16)
    here = lanes_of((16, 128)) // 8 == rows_of((16, 128))

    def as_row(part):
        wide = dot_nn(part.astype(F32).astype(BF16), spread)
        return jnp.sum(jnp.where(here, wide, 0.0), axis=0, keepdims=True)

    slot_row = as_row(owner % CE)
    device_row = as_row(owner // CE).astype(jnp.int32)
    block_row = lax.rem(lax.rem(device_row, npy) + npy - py, npy)
    hits = (rows_of((16, 128)) == block_row).astype(BF16)
    earlier = (rows_of((128, 128)) < lanes_of((128, 128))).astype(BF16)
    rank = jnp.sum(hits.astype(F32) * dot_nn(hits, earlier), axis=0, keepdims=True)
    place_row = block_row.astype(F32) * most + rank
    placed = rows_of((SLOTS, 128)).astype(F32) == place_row
    asked = jnp.sum(jnp.where(placed, slot_row + 1.0, 0.0), axis=1, keepdims=True) - 1.0
    asked = jnp.broadcast_to(asked.astype(jnp.int32), (SLOTS, 128)).reshape(npy, most, 128)
    req[...] = asked
    wanted[0] = asked[0]
    parent = (lanes_of((128, 512)) // 32) * 8 + (lanes_of((128, 512)) % 16) // 2
    family = (parent == rows_of((128, 512))).astype(BF16)
    place_wide = dot_nn(jnp.broadcast_to(place_row, (8, 128)).astype(BF16), family)[0:1]
    SEL[...] = (rows_of((SLOTS, 512)).astype(F32) == place_wide).astype(BF16)

    pl.semaphore_wait(barrier, npy + 1)

    req_copies = [None] + [
        remote(req.at[d], wanted.at[d], req_s.at[d], req_r.at[d], up[d]) for d in range(1, npy)
    ]
    for copy in req_copies[1:]:
        copy.start()

    def x_copies(section):
        if section == 0:
            low, high = fs.at[:, pl.ds(0, 40), pl.ds(0, 128)], fs.at[:, pl.ds(176, 40), pl.ds(384, 128)]
        else:
            low, high = Q.at[0, :, pl.ds(0, 40)], Q.at[3, :, pl.ds(176, 40)]
        return [
            remote(low, hx.at[section, 0], h_s.at[section, 0], h_r.at[section, 0], x_left),
            remote(high, hx.at[section, 1], h_s.at[section, 1], h_r.at[section, 1], x_right),
        ]

    def y_copies(section):
        return [
            remote(hyo.at[section, 0], hy.at[section, 0], h_s.at[section, 2], h_r.at[section, 2], y_left),
            remote(hyo.at[section, 1], hy.at[section, 1], h_s.at[section, 3], h_r.at[section, 3], y_right),
        ]

    def y_trace(ref, t, v, j):
        return jnp.concatenate([ref[t, v, pl.ds(36 * i + 6 * j, 8), :] for i in range(6)], axis=0)

    def pack_y(section):
        residue = lanes_of((48, 128)) % 16
        for v in range(5):
            low = y_trace(Q, 0, v, 0)
            high = pltpu.roll(y_trace(Q, 0, v, 5), 113, 1)
            for t in range(1, 4):
                low = jnp.where(residue == t, pltpu.roll(y_trace(Q, t, v, 0), t, 1), low)
                high = jnp.where(residue == t, pltpu.roll(y_trace(Q, t, v, 5), 113 + t, 1), high)
            hyo[section, 0, v] = low
            hyo[section, 1, v] = high

    def volume(pair, scale):
        def chunk(c, carry):
            row = pl.multiple_of(c * 16, 16)
            for side in range(2):
                r, m1, m2, m3, e = [Q[2 * pair + side, v, pl.ds(row, 16), :] for v in range(5)]
                inverse = 1.0 / r
                u1, u2, u3 = m1 * inverse, m2 * inverse, m3 * inverse
                p = pressure_of((r, m1, m2, m3, e), inverse)
                t12, t13, t23 = m2 * u1, m3 * u1, m3 * u2
                h = e + p
                for value, uses in (
                    (m1, ((0, 0),)), (m2, ((0, 1),)), (m3, ((0, 2),)),
                    (m1 * u1 + p, ((1, 0),)), (m2 * u2 + p, ((2, 1),)), (m3 * u3 + p, ((3, 2),)),
                    (t12, ((2, 0), (1, 1))), (t13, ((3, 0), (1, 2))), (t23, ((3, 1), (2, 2))),
                    (h * u1, ((4, 0),)), (h * u2, ((4, 1),)), (h * u3, ((4, 2),)),
                ):
                    high, low = split(value)
                    for v, d in uses:
                        at = pl.multiple_of(d * ROWS + row, 16)
                        FB[v, pl.ds(at, 16), pl.ds(128 * side, 128)] = high
                        FB[v, pl.ds(KH + at, 16), pl.ds(128 * side, 128)] = low
            return carry

        lax.fori_loop(0, ROWS // 16, chunk, 0)

        def one(v, carry):
            total = dot_nn(dh[...], FB[v]) + dot_nn(dl[...], FB[v, pl.ds(0, KH), :])
            R[2 * pair, v] = total[:, :128] * scale
            R[2 * pair + 1, v] = total[:, 128:] * scale
            return carry

        lax.fori_loop(0, 5, one, 0)

    def bottom(t):
        return [Q[t, v, pl.ds(0, 36, stride=6), :] for v in range(5)]

    def coarse_own():
        for t in (4, 5):
            parts = flux(bottom(t), 2)[0]
            for v in range(5):
                at = pl.ds(0, 36, stride=6)
                R[t, v, at, :] = R[t, v, at, :] - lift * parts[v]

    def x_faces(section):
        lane = lanes_of((36, 128))

        def minus(t):
            if t == 4:
                return [hx[section, 0, v, pl.ds(0, 36), :] for v in range(5)]
            return [Q[t, v, pl.ds(0, 36), :] for v in range(5)]

        def plus(t):
            if t < 0:
                return [hx[section, 1, v, pl.ds(4, 36), :] for v in range(5)]
            return [Q[t, v, pl.ds(180, 36), :] for v in range(5)]

        before = [pltpu.roll(x, 16, 1) for x in plus(-1)]
        held = None
        for t in range(5):
            right = minus(t)
            if t < 4:
                mine = [pltpu.roll(x, 16, 1) for x in plus(t)]
                left = [jnp.where(lane < 16, b, m) for b, m in zip(before, mine)]
                before = mine
            else:
                left = before
            lf, ls = flux_speed(left, 0)
            rf, rs = flux_speed(right, 0)
            low = blend(left, lf, ls, right, rf, rs)
            if t < 4:
                for v in range(5):
                    at = pl.ds(0, 36)
                    R[t, v, at, :] = R[t, v, at, :] + lift2 * (low[v] - rf[v])
            turned = [pltpu.roll(x, 112, 1) for x in low]
            if t > 0:
                own_flux = flux(plus(t - 1), 0)[0]
                for v in range(5):
                    high = jnp.where(lane >= 112, turned[v], held[v])
                    at = pl.ds(180, 36)
                    R[t - 1, v, at, :] = R[t - 1, v, at, :] + lift2 * (own_flux[v] - high)
            held = turned

    def y_faces(section):
        residue = lanes_of((48, 128)) % 16
        edge_left = [hyo[section, 1, v] for v in range(5)]
        edge_right = [hy[section, 0, v] for v in range(5)]
        lf, ls = flux_speed(edge_left, 1)
        rf, rs = flux_speed(edge_right, 1)
        edge = blend(edge_left, lf, ls, edge_right, rf, rs)
        for t in range(4):
            right = [y_trace(Q, t, v, 0) for v in range(5)]
            upper = [y_trace(Q, t, v, 5) for v in range(5)]
            left = [
                jnp.where(
                    residue == 0,
                    pltpu.roll(hy[section, 1, v], (128 - t) % 128, 1),
                    pltpu.roll(upper[v], 1, 1),
                )
                for v in range(5)
            ]
            lf, ls = flux_speed(left, 1)
            rf, rs = flux_speed(right, 1)
            low = blend(left, lf, ls, right, rf, rs)
            own_flux = flux(upper, 1)[0]
            for v in range(5):
                high = jnp.where(residue == 15, pltpu.roll(edge[v], 15 - t, 1), pltpu.roll(low[v], 127, 1))
                down_term = lift2 * (low[v] - rf[v])
                up_term = lift2 * (own_flux[v] - high)
                for i in range(6):
                    at = pl.ds(36 * i, 6)
                    R[t, v, at, :] = R[t, v, at, :] + down_term[8 * i : 8 * i + 6]
                    at = pl.ds(36 * i + 30, 6)
                    R[t, v, at, :] = R[t, v, at, :] + up_term[8 * i : 8 * i + 6]

    def ground():
        for t in range(4):
            q = bottom(t)
            parts, speed = flux_speed(q, 2)
            change = [parts[0], parts[1], parts[2], speed * q[3], parts[4]]
            for v in range(5):
                at = pl.ds(0, 36, stride=6)
                R[t, v, at, :] = R[t, v, at, :] - lift2 * change[v]

    def pick(wide, t):
        lane = lanes_of((36, 128))
        odd_a = (lane // 16) % 2 == 1
        odd_b = lane % 2 == 1
        part = [wide[40 * g : 40 * g + 36, 128 * t : 128 * t + 128] for g in range(4)]
        return jnp.where(odd_a, jnp.where(odd_b, part[3], part[2]), jnp.where(odd_b, part[1], part[0]))

    def mortar(section):
        lifted = []
        for v in range(5):
            rows = pl.ds(36 * v, 48)
            coarse_trace = jnp.concatenate([S[0, rows, :], S[1, rows, :]], axis=1)
            both = jnp.concatenate(split(coarse_trace), axis=0)
            wide = dot_nn(both, SEL[...]).astype(BF16)
            stack = jnp.concatenate([wide, wide[:48]], axis=0)
            lifted.append(dot_nn(pst[...], stack))
        for t in range(4):
            left = [Q[t, v, pl.ds(5, 36, stride=6), :] for v in range(5)]
            right = [pick(lifted[v], t) for v in range(5)]
            lf, ls = flux_speed(left, 2)
            rf, rs = flux_speed(right, 2)
            upper = blend(left, lf, ls, right, rf, rs)
            for v in range(5):
                TOPC[t, v, pl.ds(0, 36), :] = lift2 * (lf[v] - upper[v])
                MS[t, v, pl.ds(0, 36), :] = upper[v]
        for v in range(5):
            whole = jnp.concatenate([MS[t, v] for t in range(4)], axis=1)
            high, low = split(whole)
            wide = dot_nn(qst[...], jnp.concatenate([high, low, high], axis=0))
            for t in range(4):
                PM[t, pl.ds(36 * v, 36), :] = pick(wide, t)
        high, low = split(jnp.concatenate([PM[t] for t in range(4)], axis=1))
        sent = dot_nt(SEL[...], high) + dot_nt(SEL[...], low)
        sent = sent.reshape(npy, most, 256)
        fout[section] = sent
        fin[section, 0] = sent[0]
        for copy in f_copies[section][1:]:
            copy.start()
        if section == 0:
            face = dot_nt(high, SEL[...]) + dot_nt(low, SEL[...])
            for t in range(2):
                rows = pl.ds(0, 184)
                S[t, rows, :] = S[t, rows, :] + section_coefs[0][1] * (
                    S[t, pl.ds(184, 184), :] + lift * face[:184, 128 * t : 128 * t + 128]
                )

    f_copies = [
        [None]
        + [
            remote(fout.at[s, d], fin.at[s, d], f_s.at[s, d], f_r.at[s, d], up[d])
            for d in range(1, npy)
        ]
        for s in range(2)
    ]

    def fine_update(section):
        decay, step = section_coefs[section]
        for t in range(4):
            for v in range(5):
                at = pl.ds(5, 36, stride=6)
                R[t, v, at, :] = R[t, v, at, :] + TOPC[t, v, pl.ds(0, 36), :]

        def one(v, carry):
            for t in range(4):
                new = decay * G[t, v] + R[t, v, pl.ds(0, NODES), :]
                G[t, v] = new
                rows = pl.ds(0, NODES)
                Q[t, v, rows, :] = Q[t, v, rows, :] + step * new
            return carry

        lax.fori_loop(0, 5, one, 0)

    count = cnt[0]

    def coarse_update(section):
        decay, step = section_coefs[section]
        for copy in f_copies[section][1:]:
            copy.wait_recv()
        arrived = fin[section].reshape(SLOTS, 256).T
        high, low = split(arrived[:184])
        face = dot_nn(high, W[...]) + dot_nn(low, W[...])
        for t in range(2):
            for v in range(5):
                at = pl.ds(0, 36, stride=6)
                R[4 + t, v, at, :] = (
                    R[4 + t, v, at, :] + lift * face[36 * v : 36 * v + 36, 128 * t : 128 * t + 128]
                )

        def one(v, carry):
            for t in range(2):
                live = lanes_of((NODES, 128)) + 128 * t < count
                rows = pl.ds(0, NODES)
                old = G[4 + t, v]
                new = jnp.where(live, decay * old + R[4 + t, v, rows, :], old)
                G[4 + t, v] = new
                state = Q[4 + t, v, rows, :]
                Q[4 + t, v, rows, :] = jnp.where(live, state + step * new, state)
            return carry

        lax.fori_loop(0, 5, one, 0)

    x_sends = [x_copies(0), x_copies(1)]
    y_sends = [y_copies(0), y_copies(1)]
    for copy in x_sends[0]:
        copy.start()
    for t in range(4):
        loads[t].wait()
    pack_y(0)
    for copy in y_sends[0]:
        copy.start()
    for t in (4, 5, 10, 11):
        loads[t].wait()
    volume(2, -dt)
    coarse_own()
    at = pl.ds(0, 36, stride=6)
    for t in range(2):
        for v in range(5):
            BB[t, pl.ds(36 * v, 36), :] = Q[4 + t, v, at, :]
            BB[t, pl.ds(184 + 36 * v, 36), :] = section_coefs[0][0] * G[4 + t, v, at, :] + R[4 + t, v, at, :]
    for copy in req_copies[1:]:
        copy.wait_recv()
    want = wanted[...].reshape(SLOTS, 128)
    number = lanes_of((SLOTS, 128))
    W[...] = jnp.concatenate([want == number, want == number + 128], axis=1).astype(BF16)
    high, low = split(jnp.concatenate([BB[0], BB[1]], axis=1))
    reply = (dot_nt(W[...], high) + dot_nt(W[...], low)).reshape(npy, most, 384)
    rep[...] = reply
    inc[0] = reply[0]
    rep_copies = [None] + [
        remote(rep.at[d], inc.at[d], rep_s.at[d], rep_r.at[d], down[d]) for d in range(1, npy)
    ]
    for copy in rep_copies[1:]:
        copy.start()
    volume(0, -2.0 * dt)
    volume(1, -2.0 * dt)
    ground()
    for copy in x_sends[0] + y_sends[0]:
        copy.wait_recv()
    x_faces(0)
    y_faces(0)
    for copy in rep_copies[1:]:
        copy.wait_recv()
    received = inc[...].reshape(SLOTS, 384).T
    S[0] = received[:, :128]
    S[1] = received[:, 128:]
    mortar(0)
    for t in range(6, 10):
        loads[t].wait()
    fine_update(0)

    pack_y(1)
    for copy in x_sends[1] + y_sends[1]:
        copy.start()
    mortar(1)
    coarse_update(0)
    volume(2, -dt)
    coarse_own()
    volume(0, -2.0 * dt)
    volume(1, -2.0 * dt)
    ground()
    for copy in x_sends[1] + y_sends[1]:
        copy.wait_recv()
    x_faces(1)
    y_faces(1)
    for copy in x_sends[1]:
        copy.wait_send()
    fine_update(1)
    stores = []
    for t in range(6):
        lane = 128 * (t if t < 4 else t - 4)
        stores.append(
            pltpu.make_async_copy(
                Q.at[t, :, pl.ds(0, NODES)], (ofs if t < 4 else ocs).at[:, :, pl.ds(lane, 128)], out_sem.at[t]
            )
        )
        stores.append(
            pltpu.make_async_copy(
                G.at[t], (ofr if t < 4 else ocr).at[:, :, pl.ds(lane, 128)], out_sem.at[6 + t]
            )
        )
    for copy in stores[:8]:
        copy.start()
    coarse_update(1)
    for copy in stores[8:]:
        copy.start()
    for copy in req_copies[1:] + rep_copies[1:] + f_copies[0][1:] + f_copies[1][1:]:
        copy.wait_send()
    for copy in x_sends[0] + y_sends[0] + y_sends[1]:
        copy.wait_send()
    for copy in stores:
        copy.wait()


def body(shape, fine_state, fine_register, coarse_state, coarse_register, coarse_owner, coarse_count):
    npx, npy = shape
    most = SLOTS // npy
    dh, dl, pst, qst, lifting = make_tables()
    anyspace = pl.BlockSpec(memory_space=pl.ANY)
    vmem = pl.BlockSpec(memory_space=pltpu.VMEM)
    dma = pltpu.SemaphoreType.DMA
    fine = jax.ShapeDtypeStruct((5, NODES, EX * EY), F32)
    coarse = jax.ShapeDtypeStruct((5, NODES, CE), F32)
    return pl.pallas_call(
        functools.partial(kernel, shape, lifting),
        out_shape=(fine, fine, coarse, coarse),
        in_specs=[anyspace] * 4 + [vmem, pl.BlockSpec(memory_space=pltpu.SMEM)] + [vmem] * 4,
        out_specs=(anyspace,) * 4,
        scratch_shapes=[
            pltpu.VMEM((6, 5, ROWS, 128), F32),
            pltpu.VMEM((6, 5, NODES, 128), F32),
            pltpu.VMEM((6, 5, ROWS, 128), F32),
            pltpu.VMEM((5, 2 * KH, 256), BF16),
            pltpu.VMEM((2, 384, 128), F32),
            pltpu.VMEM((2, 384, 128), F32),
            pltpu.VMEM((SLOTS, CE), BF16),
            pltpu.VMEM((SLOTS, 512), BF16),
            pltpu.VMEM((4, 5, 48, 128), F32),
            pltpu.VMEM((4, 256, 128), F32),
            pltpu.VMEM((4, 5, 40, 128), F32),
            pltpu.VMEM((npy, most, 128), jnp.int32),
            pltpu.VMEM((npy, most, 128), jnp.int32),
            pltpu.VMEM((npy, most, 384), F32),
            pltpu.VMEM((npy, most, 384), F32),
            pltpu.VMEM((2, npy, most, 256), F32),
            pltpu.VMEM((2, npy, most, 256), F32),
            pltpu.VMEM((2, 2, 5, 40, 128), F32),
            pltpu.VMEM((2, 2, 5, 48, 128), F32),
            pltpu.VMEM((2, 2, 5, 48, 128), F32),
            dma((12,)),
            dma((12,)),
            dma((npy,)),
            dma((npy,)),
            dma((npy,)),
            dma((npy,)),
            dma((2, npy)),
            dma((2, npy)),
            dma((2, 4)),
            dma((2, 4)),
        ],
        compiler_params=pltpu.CompilerParams(
            collective_id=0, has_side_effects=True, vmem_limit_bytes=56 << 20
        ),
    )(
        fine_state, fine_register, coarse_state, coarse_register, coarse_owner, coarse_count,
        jnp.asarray(dh), jnp.asarray(dl), jnp.asarray(pst), jnp.asarray(qst),
    )


def solution(mesh):
    whole = P(None, None, ("px", "py"))
    return jax.shard_map(
        functools.partial(body, (mesh.shape["px"], mesh.shape["py"])),
        mesh=mesh,
        in_specs=(whole, whole, whole, whole, P("px", "py"), P(("px", "py"))),
        out_specs=(whole,) * 4,
        check_vma=False,
    )
```

```python
import functools
import math

import jax
import jax.numpy as jnp
import numpy as np
from jax import lax
from jax.experimental import pallas as pl
from jax.experimental.pallas import tpu as pltpu
from jax.sharding import PartitionSpec as P

NP = 6
NODES = 216
ROWS = 224
EX = 32
EY = 16
CE = 256
SLOTS = 256

time_step = 0.01
section_coefs = ((-0.4178904745, 0.3792103129), (-1.192151694643, 0.8229550293869))
MESH = pl.DeviceIdType.MESH
F32 = jnp.float32
BF16 = jnp.bfloat16


def legendre_columns(nodes, points):
    columns = [np.ones(points), nodes]
    for degree in range(2, points):
        columns.append(
            ((2 * degree - 1) * nodes * columns[-1] - (degree - 1) * columns[-2]) / degree
        )
    return columns


def node_tables(points):
    order = points - 1
    nodes = np.array([-math.cos(math.pi * index / order) for index in range(points)])
    for sweep in range(60):
        columns = legendre_columns(nodes, points)
        nodes = nodes - (nodes * columns[order] - columns[order - 1]) / (points * columns[order])
    legendre = legendre_columns(nodes, points)[order]
    weights = 2.0 / (order * points * legendre**2)
    same = np.arange(points)[:, None] == np.arange(points)[None, :]
    spread = nodes[:, None] - nodes[None, :] + np.where(same, 1.0, 0.0)
    barycentric = 1.0 / np.prod(spread, axis=1)
    derivative = np.where(same, 0.0, barycentric[None, :] / barycentric[:, None] / spread)
    derivative = derivative - np.where(same, np.sum(derivative, axis=1)[:, None], 0.0)
    halves = []
    for side in (-1.0, 1.0):
        target = 0.5 * (nodes + side)
        table = np.ones((points, points))
        for column in range(points):
            for other in range(points):
                if other != column:
                    table[:, column] *= (target - nodes[other]) / (nodes[column] - nodes[other])
        halves.append(table)
    to_fine = np.stack(halves)
    to_coarse = 0.5 * to_fine.transpose(0, 2, 1) * weights[None, None, :] / weights[None, :, None]
    f = np.float32
    return derivative, to_fine.astype(f), to_coarse.astype(f), float(1.0 / weights[0])


def halves_of(table):
    high = np.asarray(table, np.float32).astype(BF16)
    low = (np.asarray(table, np.float32) - high.astype(np.float32)).astype(BF16)
    return high, low


def make_tables():
    derivative, to_fine, to_coarse, lifting = node_tables(NP)
    even_table = 0.5 * (derivative[:3, :3] + derivative[:3, 5:2:-1])
    odd_table = 0.5 * (derivative[:3, :3] - derivative[:3, 5:2:-1])
    stacks = []
    for table in (to_fine, to_coarse):
        full = np.zeros((160, 48), np.float32)
        for a in range(2):
            for b in range(2):
                r = (2 * a + b) * 40
                full[r : r + 36, :36] = np.kron(table[a], table[b])
        th, tl = halves_of(full)
        stacks.append(np.concatenate([th, th, tl], axis=1))
    return even_table, odd_table, stacks[0], stacks[1], lifting


PAIRS = {(0, 0): 0, (0, 1): 1, (0, 2): 2, (1, 0): 1, (1, 1): 3, (1, 2): 4, (2, 0): 2, (2, 1): 4, (2, 2): 5}


def lines(d):
    sizes = (8, 8, 8, 8, 4)
    if d == 0:
        return [[pl.ds(36 * i + 8 * c, sizes[c]) for i in range(6)] for c in range(5)]
    if d == 1:
        return [[pl.ds(36 * i + 6 * j, 6) for j in range(6)] for i in range(6)]
    return [[pl.ds(48 * c + k, sizes[c], stride=6) for k in range(6)] for c in range(5)]


def split(x):
    high = x.astype(BF16)
    low = (x - high.astype(F32)).astype(BF16)
    return high, low


def dot_nn(a, b):
    return lax.dot_general(a, b, (((1,), (0,)), ((), ())), preferred_element_type=F32)


def dot_nt(a, b):
    return lax.dot_general(a, b, (((1,), (1,)), ((), ())), preferred_element_type=F32)


def pressure_of(q, inverse):
    return 0.4 * (q[4] - 0.5 * (q[1] * q[1] + q[2] * q[2] + q[3] * q[3]) * inverse)


def flux(q, d):
    inverse = 1.0 / q[0]
    velocity = q[1 + d] * inverse
    pressure = pressure_of(q, inverse)
    parts = [q[1 + d], q[1] * velocity, q[2] * velocity, q[3] * velocity, (q[4] + pressure) * velocity]
    parts[1 + d] = parts[1 + d] + pressure
    return parts, velocity, pressure, inverse


def flux_speed(q, d):
    parts, velocity, pressure, inverse = flux(q, d)
    return parts, jnp.abs(velocity) + jnp.sqrt(1.4 * pressure * inverse)


def blend(left, left_flux, left_speed, right, right_flux, right_speed):
    fastest = 0.5 * jnp.maximum(left_speed, right_speed)
    return [
        0.5 * (lf + rf) - fastest * (r - l)
        for l, lf, r, rf in zip(left, left_flux, right, right_flux)
    ]


def lanes_of(shape):
    return lax.broadcasted_iota(jnp.int32, shape, len(shape) - 1)


def rows_of(shape):
    return lax.broadcasted_iota(jnp.int32, shape, len(shape) - 2)


def kernel(
    shape, lifting, even_table, odd_table,
    fs, fr, cs, cr, own, cnt, pst, qst,
    ofs, ofr, ocs, ocr,
    Q, G, R, FX, BB, S, W, SEL, MS, PM, TOPC,
    req, wanted, rep, inc, fout, fin, hx, hyo, hy,
    in_sem, out_sem, req_s, req_r, rep_s, rep_r, f_s, f_r, h_s, h_r,
):
    npx, npy = shape
    most = SLOTS // npy
    px = lax.axis_index("px")
    py = lax.axis_index("py")
    up = [(px, lax.rem(py + d, npy)) for d in range(npy)]
    down = [(px, lax.rem(py + npy - d, npy)) for d in range(npy)]
    x_right, x_left = (lax.rem(px + 1, npx), py), (lax.rem(px + npx - 1, npx), py)
    y_right, y_left = up[1], down[1]
    dt = time_step
    lift = dt * lifting
    lift2 = 2.0 * lift

    def remote(src, dst, ss, rs, dev):
        return pltpu.make_async_remote_copy(
            src_ref=src, dst_ref=dst, send_sem=ss, recv_sem=rs, device_id=dev, device_id_type=MESH
        )

    barrier = pltpu.get_barrier_semaphore()
    for d in range(1, npy):
        pl.semaphore_signal(barrier, inc=1, device_id=up[d], device_id_type=MESH)
    pl.semaphore_signal(barrier, inc=1, device_id=x_right, device_id_type=MESH)
    pl.semaphore_signal(barrier, inc=1, device_id=x_left, device_id_type=MESH)

    loads = []
    for t in range(6):
        src = fs if t < 4 else cs
        lane = 128 * (t if t < 4 else t - 4)
        loads.append(
            pltpu.make_async_copy(src.at[:, :, pl.ds(lane, 128)], Q.at[t, :, pl.ds(0, NODES)], in_sem.at[t])
        )
    for t in range(6):
        src = fr if t < 4 else cr
        lane = 128 * (t if t < 4 else t - 4)
        loads.append(
            pltpu.make_async_copy(src.at[:, :, pl.ds(lane, 128)], G.at[t], in_sem.at[6 + t])
        )
    for copy in loads:
        copy.start()

    for t in range(6):
        for v in range(5):
            Q[t, v, pl.ds(NODES, ROWS - NODES), :] = jnp.full(
                (ROWS - NODES, 128), (1.0, 0.0, 0.0, 0.0, 2.5)[v], F32
            )
    for t in range(2):
        BB[t, pl.ds(180, 4), :] = jnp.zeros((4, 128), F32)
        BB[t, pl.ds(364, 20), :] = jnp.zeros((20, 128), F32)
    for t in range(4):
        PM[t, pl.ds(180, 76), :] = jnp.zeros((76, 128), F32)
        for v in range(5):
            MS[t, v, pl.ds(36, 12), :] = jnp.zeros((12, 128), F32)

    owner = own[...]
    spread = (lanes_of((8, 128)) % 8 == rows_of((8, 128))).astype(BF16)
    here = lanes_of((16, 128)) // 8 == rows_of((16, 128))

    def as_row(part):
        wide = dot_nn(part.astype(F32).astype(BF16), spread)
        return jnp.sum(jnp.where(here, wide, 0.0), axis=0, keepdims=True)

    slot_row = as_row(owner % CE)
    device_row = as_row(owner // CE).astype(jnp.int32)
    block_row = lax.rem(lax.rem(device_row, npy) + npy - py, npy)
    hits = (rows_of((16, 128)) == block_row).astype(BF16)
    earlier = (rows_of((128, 128)) < lanes_of((128, 128))).astype(BF16)
    rank = jnp.sum(hits.astype(F32) * dot_nn(hits, earlier), axis=0, keepdims=True)
    place_row = block_row.astype(F32) * most + rank
    placed = rows_of((SLOTS, 128)).astype(F32) == place_row
    asked = jnp.sum(jnp.where(placed, slot_row + 1.0, 0.0), axis=1, keepdims=True) - 1.0
    asked = jnp.broadcast_to(asked.astype(jnp.int32), (SLOTS, 128)).reshape(npy, most, 128)
    req[...] = asked
    wanted[0] = asked[0]
    parent = (lanes_of((128, 512)) // 32) * 8 + (lanes_of((128, 512)) % 16) // 2
    family = (parent == rows_of((128, 512))).astype(BF16)
    place_wide = dot_nn(jnp.broadcast_to(place_row, (8, 128)).astype(BF16), family)[0:1]
    SEL[...] = (rows_of((SLOTS, 512)).astype(F32) == place_wide).astype(BF16)

    pl.semaphore_wait(barrier, npy + 1)

    req_copies = [None] + [
        remote(req.at[d], wanted.at[d], req_s.at[d], req_r.at[d], up[d]) for d in range(1, npy)
    ]
    for copy in req_copies[1:]:
        copy.start()

    def x_copies(section):
        if section == 0:
            low, high = fs.at[:, pl.ds(0, 40), pl.ds(0, 128)], fs.at[:, pl.ds(176, 40), pl.ds(384, 128)]
        else:
            low, high = Q.at[0, :, pl.ds(0, 40)], Q.at[3, :, pl.ds(176, 40)]
        return [
            remote(low, hx.at[section, 0], h_s.at[section, 0], h_r.at[section, 0], x_left),
            remote(high, hx.at[section, 1], h_s.at[section, 1], h_r.at[section, 1], x_right),
        ]

    def y_copies(section):
        return [
            remote(hyo.at[section, 0], hy.at[section, 0], h_s.at[section, 2], h_r.at[section, 2], y_left),
            remote(hyo.at[section, 1], hy.at[section, 1], h_s.at[section, 3], h_r.at[section, 3], y_right),
        ]

    def y_trace(ref, t, v, j):
        return jnp.concatenate([ref[t, v, pl.ds(36 * i + 6 * j, 8), :] for i in range(6)], axis=0)

    def pack_y(section):
        residue = lanes_of((48, 128)) % 16
        for v in range(5):
            low = y_trace(Q, 0, v, 0)
            high = pltpu.roll(y_trace(Q, 0, v, 5), 113, 1)
            for t in range(1, 4):
                low = jnp.where(residue == t, pltpu.roll(y_trace(Q, t, v, 0), t, 1), low)
                high = jnp.where(residue == t, pltpu.roll(y_trace(Q, t, v, 5), 113 + t, 1), high)
            hyo[section, 0, v] = low
            hyo[section, 1, v] = high

    def volume(first, last, scale):
        def tile(t, carry):
            def chunk(c, inner):
                rows = pl.ds(pl.multiple_of(c * 24, 8), 24)
                r, m1, m2, m3, e = [Q[t, v, rows, :] for v in range(5)]
                inverse = 1.0 / r
                u1, u2, u3 = m1 * inverse, m2 * inverse, m3 * inverse
                p = pressure_of((r, m1, m2, m3, e), inverse)
                h = e + p
                for s, value in enumerate(
                    (m1 * u1 + p, m2 * u1, m3 * u1, m2 * u2 + p, m3 * u2, m3 * u3 + p, h * u1, h * u2, h * u3)
                ):
                    FX[t, s, rows, :] = value
                return inner

            lax.fori_loop(0, NODES // 24, chunk, 0)
            for v in range(5):
                for d in range(3):
                    flow = Q.at[t, 1 + d] if v == 0 else FX.at[t, 6 + d if v == 4 else PAIRS[(v - 1, d)]]
                    for spans in lines(d):
                        out = differ([flow[at, :] for at in spans], scale)
                        for at, value in zip(spans, out):
                            if d == 0:
                                R[t, v, at, :] = value
                            else:
                                R[t, v, at, :] = R[t, v, at, :] + value
            return carry

        lax.fori_loop(first, last, tile, 0)

    def differ(f, scale):
        even = [f[j] + f[5 - j] for j in range(3)]
        odd = [f[j] - f[5 - j] for j in range(3)]
        first, second = even[0] - even[2], even[1] - even[2]
        out = [None] * 6
        for i in range(3):
            a = float(scale * even_table[i, 0]) * first + float(scale * even_table[i, 1]) * second
            b = float(scale * odd_table[i, 0]) * odd[0] + float(scale * odd_table[i, 1]) * odd[1]
            b = b + float(scale * odd_table[i, 2]) * odd[2]
            out[i], out[5 - i] = b + a, b - a
        return out

    def bottom(t):
        return [Q[t, v, pl.ds(0, 36, stride=6), :] for v in range(5)]

    def coarse_own():
        for t in (4, 5):
            parts = flux(bottom(t), 2)[0]
            for v in range(5):
                at = pl.ds(0, 36, stride=6)
                R[t, v, at, :] = R[t, v, at, :] - lift * parts[v]

    def x_faces(section):
        lane = lanes_of((36, 128))

        def minus(t):
            if t == 4:
                return [hx[section, 0, v, pl.ds(0, 36), :] for v in range(5)]
            return [Q[t, v, pl.ds(0, 36), :] for v in range(5)]

        def plus(t):
            if t < 0:
                return [hx[section, 1, v, pl.ds(4, 36), :] for v in range(5)]
            return [Q[t, v, pl.ds(180, 36), :] for v in range(5)]

        before = [pltpu.roll(x, 16, 1) for x in plus(-1)]
        held = None
        for t in range(5):
            right = minus(t)
            if t < 4:
                mine = [pltpu.roll(x, 16, 1) for x in plus(t)]
                left = [jnp.where(lane < 16, b, m) for b, m in zip(before, mine)]
                before = mine
            else:
                left = before
            lf, ls = flux_speed(left, 0)
            rf, rs = flux_speed(right, 0)
            low = blend(left, lf, ls, right, rf, rs)
            if t < 4:
                for v in range(5):
                    at = pl.ds(0, 36)
                    R[t, v, at, :] = R[t, v, at, :] + lift2 * (low[v] - rf[v])
            turned = [pltpu.roll(x, 112, 1) for x in low]
            if t > 0:
                own_flux = flux(plus(t - 1), 0)[0]
                for v in range(5):
                    high = jnp.where(lane >= 112, turned[v], held[v])
                    at = pl.ds(180, 36)
                    R[t - 1, v, at, :] = R[t - 1, v, at, :] + lift2 * (own_flux[v] - high)
            held = turned

    def y_faces(section):
        residue = lanes_of((48, 128)) % 16
        edge_left = [hyo[section, 1, v] for v in range(5)]
        edge_right = [hy[section, 0, v] for v in range(5)]
        lf, ls = flux_speed(edge_left, 1)
        rf, rs = flux_speed(edge_right, 1)
        edge = blend(edge_left, lf, ls, edge_right, rf, rs)
        for t in range(4):
            right = [y_trace(Q, t, v, 0) for v in range(5)]
            upper = [y_trace(Q, t, v, 5) for v in range(5)]
            left = [
                jnp.where(
                    residue == 0,
                    pltpu.roll(hy[section, 1, v], (128 - t) % 128, 1),
                    pltpu.roll(upper[v], 1, 1),
                )
                for v in range(5)
            ]
            lf, ls = flux_speed(left, 1)
            rf, rs = flux_speed(right, 1)
            low = blend(left, lf, ls, right, rf, rs)
            own_flux = flux(upper, 1)[0]
            for v in range(5):
                high = jnp.where(residue == 15, pltpu.roll(edge[v], 15 - t, 1), pltpu.roll(low[v], 127, 1))
                down_term = lift2 * (low[v] - rf[v])
                up_term = lift2 * (own_flux[v] - high)
                for i in range(6):
                    at = pl.ds(36 * i, 6)
                    R[t, v, at, :] = R[t, v, at, :] + down_term[8 * i : 8 * i + 6]
                    at = pl.ds(36 * i + 30, 6)
                    R[t, v, at, :] = R[t, v, at, :] + up_term[8 * i : 8 * i + 6]

    def ground():
        for t in range(4):
            q = bottom(t)
            parts, speed = flux_speed(q, 2)
            change = [parts[0], parts[1], parts[2], speed * q[3], parts[4]]
            for v in range(5):
                at = pl.ds(0, 36, stride=6)
                R[t, v, at, :] = R[t, v, at, :] - lift2 * change[v]

    def pick(wide, t):
        lane = lanes_of((36, 128))
        odd_a = (lane // 16) % 2 == 1
        odd_b = lane % 2 == 1
        part = [wide[40 * g : 40 * g + 36, 128 * t : 128 * t + 128] for g in range(4)]
        return jnp.where(odd_a, jnp.where(odd_b, part[3], part[2]), jnp.where(odd_b, part[1], part[0]))

    def mortar(section):
        lifted = []
        for v in range(5):
            rows = pl.ds(36 * v, 48)
            coarse_trace = jnp.concatenate([S[0, rows, :], S[1, rows, :]], axis=1)
            both = jnp.concatenate(split(coarse_trace), axis=0)
            wide = dot_nn(both, SEL[...]).astype(BF16)
            stack = jnp.concatenate([wide, wide[:48]], axis=0)
            lifted.append(dot_nn(pst[...], stack))
        for t in range(4):
            left = [Q[t, v, pl.ds(5, 36, stride=6), :] for v in range(5)]
            right = [pick(lifted[v], t) for v in range(5)]
            lf, ls = flux_speed(left, 2)
            rf, rs = flux_speed(right, 2)
            upper = blend(left, lf, ls, right, rf, rs)
            for v in range(5):
                TOPC[t, v, pl.ds(0, 36), :] = lift2 * (lf[v] - upper[v])
                MS[t, v, pl.ds(0, 36), :] = upper[v]
        for v in range(5):
            whole = jnp.concatenate([MS[t, v] for t in range(4)], axis=1)
            high, low = split(whole)
            wide = dot_nn(qst[...], jnp.concatenate([high, low, high], axis=0))
            for t in range(4):
                PM[t, pl.ds(36 * v, 36), :] = pick(wide, t)
        high, low = split(jnp.concatenate([PM[t] for t in range(4)], axis=1))
        sent = dot_nt(SEL[...], high) + dot_nt(SEL[...], low)
        sent = sent.reshape(npy, most, 256)
        fout[section] = sent
        fin[section, 0] = sent[0]
        for copy in f_copies[section][1:]:
            copy.start()
        if section == 0:
            face = dot_nt(high, SEL[...]) + dot_nt(low, SEL[...])
            for t in range(2):
                rows = pl.ds(0, 184)
                S[t, rows, :] = S[t, rows, :] + section_coefs[0][1] * (
                    S[t, pl.ds(184, 184), :] + lift * face[:184, 128 * t : 128 * t + 128]
                )

    f_copies = [
        [None]
        + [
            remote(fout.at[s, d], fin.at[s, d], f_s.at[s, d], f_r.at[s, d], up[d])
            for d in range(1, npy)
        ]
        for s in range(2)
    ]

    def fine_update(section):
        decay, step = section_coefs[section]
        for t in range(4):
            for v in range(5):
                at = pl.ds(5, 36, stride=6)
                R[t, v, at, :] = R[t, v, at, :] + TOPC[t, v, pl.ds(0, 36), :]

        def one(v, carry):
            for t in range(4):
                new = decay * G[t, v] + R[t, v, pl.ds(0, NODES), :]
                G[t, v] = new
                rows = pl.ds(0, NODES)
                Q[t, v, rows, :] = Q[t, v, rows, :] + step * new
            return carry

        lax.fori_loop(0, 5, one, 0)

    count = cnt[0]

    def coarse_update(section):
        decay, step = section_coefs[section]
        for copy in f_copies[section][1:]:
            copy.wait_recv()
        arrived = fin[section].reshape(SLOTS, 256).T
        high, low = split(arrived[:184])
        face = dot_nn(high, W[...]) + dot_nn(low, W[...])
        for t in range(2):
            for v in range(5):
                at = pl.ds(0, 36, stride=6)
                R[4 + t, v, at, :] = (
                    R[4 + t, v, at, :] + lift * face[36 * v : 36 * v + 36, 128 * t : 128 * t + 128]
                )

        def one(v, carry):
            for t in range(2):
                live = lanes_of((NODES, 128)) + 128 * t < count
                rows = pl.ds(0, NODES)
                old = G[4 + t, v]
                new = jnp.where(live, decay * old + R[4 + t, v, rows, :], old)
                G[4 + t, v] = new
                state = Q[4 + t, v, rows, :]
                Q[4 + t, v, rows, :] = jnp.where(live, state + step * new, state)
            return carry

        lax.fori_loop(0, 5, one, 0)

    x_sends = [x_copies(0), x_copies(1)]
    y_sends = [y_copies(0), y_copies(1)]
    for copy in x_sends[0]:
        copy.start()
    for t in range(4):
        loads[t].wait()
    pack_y(0)
    for copy in y_sends[0]:
        copy.start()
    for t in (4, 5, 10, 11):
        loads[t].wait()
    volume(4, 6, -dt)
    coarse_own()
    at = pl.ds(0, 36, stride=6)
    for t in range(2):
        for v in range(5):
            BB[t, pl.ds(36 * v, 36), :] = Q[4 + t, v, at, :]
            BB[t, pl.ds(184 + 36 * v, 36), :] = section_coefs[0][0] * G[4 + t, v, at, :] + R[4 + t, v, at, :]
    for copy in req_copies[1:]:
        copy.wait_recv()
    want = wanted[...].reshape(SLOTS, 128)
    number = lanes_of((SLOTS, 128))
    W[...] = jnp.concatenate([want == number, want == number + 128], axis=1).astype(BF16)
    high, low = split(jnp.concatenate([BB[0], BB[1]], axis=1))
    reply = (dot_nt(W[...], high) + dot_nt(W[...], low)).reshape(npy, most, 384)
    rep[...] = reply
    inc[0] = reply[0]
    rep_copies = [None] + [
        remote(rep.at[d], inc.at[d], rep_s.at[d], rep_r.at[d], down[d]) for d in range(1, npy)
    ]
    for copy in rep_copies[1:]:
        copy.start()
    volume(0, 4, -2.0 * dt)
    ground()
    for copy in x_sends[0] + y_sends[0]:
        copy.wait_recv()
    x_faces(0)
    y_faces(0)
    for copy in rep_copies[1:]:
        copy.wait_recv()
    received = inc[...].reshape(SLOTS, 384).T
    S[0] = received[:, :128]
    S[1] = received[:, 128:]
    mortar(0)
    for t in range(6, 10):
        loads[t].wait()
    fine_update(0)

    pack_y(1)
    for copy in x_sends[1] + y_sends[1]:
        copy.start()
    mortar(1)
    coarse_update(0)
    volume(4, 6, -dt)
    coarse_own()
    volume(0, 4, -2.0 * dt)
    ground()
    for copy in x_sends[1] + y_sends[1]:
        copy.wait_recv()
    x_faces(1)
    y_faces(1)
    for copy in x_sends[1]:
        copy.wait_send()
    fine_update(1)
    stores = []
    for t in range(6):
        lane = 128 * (t if t < 4 else t - 4)
        stores.append(
            pltpu.make_async_copy(
                Q.at[t, :, pl.ds(0, NODES)], (ofs if t < 4 else ocs).at[:, :, pl.ds(lane, 128)], out_sem.at[t]
            )
        )
        stores.append(
            pltpu.make_async_copy(
                G.at[t], (ofr if t < 4 else ocr).at[:, :, pl.ds(lane, 128)], out_sem.at[6 + t]
            )
        )
    for copy in stores[:8]:
        copy.start()
    coarse_update(1)
    for copy in stores[8:]:
        copy.start()
    for copy in req_copies[1:] + rep_copies[1:] + f_copies[0][1:] + f_copies[1][1:]:
        copy.wait_send()
    for copy in x_sends[0] + y_sends[0] + y_sends[1]:
        copy.wait_send()
    for copy in stores:
        copy.wait()


def body(shape, fine_state, fine_register, coarse_state, coarse_register, coarse_owner, coarse_count):
    npx, npy = shape
    most = SLOTS // npy
    even_table, odd_table, pst, qst, lifting = make_tables()
    anyspace = pl.BlockSpec(memory_space=pl.ANY)
    vmem = pl.BlockSpec(memory_space=pltpu.VMEM)
    dma = pltpu.SemaphoreType.DMA
    fine = jax.ShapeDtypeStruct((5, NODES, EX * EY), F32)
    coarse = jax.ShapeDtypeStruct((5, NODES, CE), F32)
    return pl.pallas_call(
        functools.partial(kernel, shape, lifting, even_table, odd_table),
        out_shape=(fine, fine, coarse, coarse),
        in_specs=[anyspace] * 4 + [vmem, pl.BlockSpec(memory_space=pltpu.SMEM)] + [vmem] * 2,
        out_specs=(anyspace,) * 4,
        scratch_shapes=[
            pltpu.VMEM((6, 5, ROWS, 128), F32),
            pltpu.VMEM((6, 5, NODES, 128), F32),
            pltpu.VMEM((6, 5, ROWS, 128), F32),
            pltpu.VMEM((6, 9, NODES, 128), F32),
            pltpu.VMEM((2, 384, 128), F32),
            pltpu.VMEM((2, 384, 128), F32),
            pltpu.VMEM((SLOTS, CE), BF16),
            pltpu.VMEM((SLOTS, 512), BF16),
            pltpu.VMEM((4, 5, 48, 128), F32),
            pltpu.VMEM((4, 256, 128), F32),
            pltpu.VMEM((4, 5, 40, 128), F32),
            pltpu.VMEM((npy, most, 128), jnp.int32),
            pltpu.VMEM((npy, most, 128), jnp.int32),
            pltpu.VMEM((npy, most, 384), F32),
            pltpu.VMEM((npy, most, 384), F32),
            pltpu.VMEM((2, npy, most, 256), F32),
            pltpu.VMEM((2, npy, most, 256), F32),
            pltpu.VMEM((2, 2, 5, 40, 128), F32),
            pltpu.VMEM((2, 2, 5, 48, 128), F32),
            pltpu.VMEM((2, 2, 5, 48, 128), F32),
            dma((12,)),
            dma((12,)),
            dma((npy,)),
            dma((npy,)),
            dma((npy,)),
            dma((npy,)),
            dma((2, npy)),
            dma((2, npy)),
            dma((2, 4)),
            dma((2, 4)),
        ],
        compiler_params=pltpu.CompilerParams(
            collective_id=0, has_side_effects=True, vmem_limit_bytes=56 << 20
        ),
    )(
        fine_state, fine_register, coarse_state, coarse_register, coarse_owner, coarse_count,
        jnp.asarray(pst), jnp.asarray(qst),
    )


def solution(mesh):
    whole = P(None, None, ("px", "py"))
    return jax.shard_map(
        functools.partial(body, (mesh.shape["px"], mesh.shape["py"])),
        mesh=mesh,
        in_specs=(whole, whole, whole, whole, P("px", "py"), P(("px", "py"))),
        out_specs=(whole,) * 4,
        check_vma=False,
    )
```

```python
import functools
import math

import jax
import jax.numpy as jnp
import numpy as np
from jax import lax
from jax.experimental import pallas as pl
from jax.experimental.pallas import tpu as pltpu
from jax.sharding import PartitionSpec as P

NP = 6
NODES = 216
ROWS = 224
EX = 32
EY = 16
CE = 256
SLOTS = 256

time_step = 0.01
section_coefs = ((-0.4178904745, 0.3792103129), (-1.192151694643, 0.8229550293869))
MESH = pl.DeviceIdType.MESH
F32 = jnp.float32
BF16 = jnp.bfloat16


def legendre_columns(nodes, points):
    columns = [np.ones(points), nodes]
    for degree in range(2, points):
        columns.append(
            ((2 * degree - 1) * nodes * columns[-1] - (degree - 1) * columns[-2]) / degree
        )
    return columns


def node_tables(points):
    order = points - 1
    nodes = np.array([-math.cos(math.pi * index / order) for index in range(points)])
    for sweep in range(60):
        columns = legendre_columns(nodes, points)
        nodes = nodes - (nodes * columns[order] - columns[order - 1]) / (points * columns[order])
    legendre = legendre_columns(nodes, points)[order]
    weights = 2.0 / (order * points * legendre**2)
    same = np.arange(points)[:, None] == np.arange(points)[None, :]
    spread = nodes[:, None] - nodes[None, :] + np.where(same, 1.0, 0.0)
    barycentric = 1.0 / np.prod(spread, axis=1)
    derivative = np.where(same, 0.0, barycentric[None, :] / barycentric[:, None] / spread)
    derivative = derivative - np.where(same, np.sum(derivative, axis=1)[:, None], 0.0)
    halves = []
    for side in (-1.0, 1.0):
        target = 0.5 * (nodes + side)
        table = np.ones((points, points))
        for column in range(points):
            for other in range(points):
                if other != column:
                    table[:, column] *= (target - nodes[other]) / (nodes[column] - nodes[other])
        halves.append(table)
    to_fine = np.stack(halves)
    to_coarse = 0.5 * to_fine.transpose(0, 2, 1) * weights[None, None, :] / weights[None, :, None]
    f = np.float32
    return derivative, to_fine.astype(f), to_coarse.astype(f), float(1.0 / weights[0])


def halves_of(table):
    high = np.asarray(table, np.float32).astype(BF16)
    low = (np.asarray(table, np.float32) - high.astype(np.float32)).astype(BF16)
    return high, low


def make_tables():
    derivative, to_fine, to_coarse, lifting = node_tables(NP)
    even_table = 0.5 * (derivative[:3, :3] + derivative[:3, 5:2:-1])
    odd_table = 0.5 * (derivative[:3, :3] - derivative[:3, 5:2:-1])
    stacks = []
    for table in (to_fine, to_coarse):
        full = np.zeros((160, 48), np.float32)
        for a in range(2):
            for b in range(2):
                r = (2 * a + b) * 40
                full[r : r + 36, :36] = np.kron(table[a], table[b])
        th, tl = halves_of(full)
        stacks.append(np.concatenate([th, th, tl], axis=1))
    return even_table, odd_table, stacks[0], stacks[1], lifting


PAIRS = {(0, 0): 0, (0, 1): 1, (0, 2): 2, (1, 0): 1, (1, 1): 3, (1, 2): 4, (2, 0): 2, (2, 1): 4, (2, 2): 5}


def lines(d):
    sizes = (8, 8, 8, 8, 4)
    if d == 0:
        return [[pl.ds(36 * i + 8 * c, sizes[c]) for i in range(6)] for c in range(5)]
    if d == 1:
        return [[pl.ds(36 * i + 6 * j, 6) for j in range(6)] for i in range(6)]
    return [[pl.ds(48 * c + k, sizes[c], stride=6) for k in range(6)] for c in range(5)]


def split(x):
    high = x.astype(BF16)
    low = (x - high.astype(F32)).astype(BF16)
    return high, low


def dot_nn(a, b):
    return lax.dot_general(a, b, (((1,), (0,)), ((), ())), preferred_element_type=F32)


def dot_nt(a, b):
    return lax.dot_general(a, b, (((1,), (1,)), ((), ())), preferred_element_type=F32)


def pressure_of(q, inverse):
    return 0.4 * (q[4] - 0.5 * (q[1] * q[1] + q[2] * q[2] + q[3] * q[3]) * inverse)


def flux(q, d):
    inverse = 1.0 / q[0]
    velocity = q[1 + d] * inverse
    pressure = pressure_of(q, inverse)
    parts = [q[1 + d], q[1] * velocity, q[2] * velocity, q[3] * velocity, (q[4] + pressure) * velocity]
    parts[1 + d] = parts[1 + d] + pressure
    return parts, velocity, pressure, inverse


def flux_speed(q, d):
    parts, velocity, pressure, inverse = flux(q, d)
    return parts, jnp.abs(velocity) + jnp.sqrt(1.4 * pressure * inverse)


def blend(left, left_flux, left_speed, right, right_flux, right_speed):
    fastest = 0.5 * jnp.maximum(left_speed, right_speed)
    return [
        0.5 * (lf + rf) - fastest * (r - l)
        for l, lf, r, rf in zip(left, left_flux, right, right_flux)
    ]


def lanes_of(shape):
    return lax.broadcasted_iota(jnp.int32, shape, len(shape) - 1)


def rows_of(shape):
    return lax.broadcasted_iota(jnp.int32, shape, len(shape) - 2)


def kernel(
    shape, lifting, even_table, odd_table,
    fs, fr, cs, cr, own, cnt, pst, qst,
    ofs, ofr, ocs, ocr,
    Q, G, R, FX, BB, S, W, SEL, MS, PM, TOPC,
    req, wanted, rep, inc, rest, incb, fout, fin, hx, hyo, hy,
    in_sem, out_sem, req_s, req_r, rep_s, rep_r, f_s, f_r, h_s, h_r,
):
    npx, npy = shape
    most = SLOTS // npy
    px = lax.axis_index("px")
    py = lax.axis_index("py")
    up = [(px, lax.rem(py + d, npy)) for d in range(npy)]
    down = [(px, lax.rem(py + npy - d, npy)) for d in range(npy)]
    x_right, x_left = (lax.rem(px + 1, npx), py), (lax.rem(px + npx - 1, npx), py)
    y_right, y_left = up[1], down[1]
    dt = time_step
    lift = dt * lifting
    lift2 = 2.0 * lift

    def remote(src, dst, ss, rs, dev):
        return pltpu.make_async_remote_copy(
            src_ref=src, dst_ref=dst, send_sem=ss, recv_sem=rs, device_id=dev, device_id_type=MESH
        )

    barrier = pltpu.get_barrier_semaphore()
    for d in range(1, npy):
        pl.semaphore_signal(barrier, inc=1, device_id=up[d], device_id_type=MESH)
    pl.semaphore_signal(barrier, inc=1, device_id=x_right, device_id_type=MESH)
    pl.semaphore_signal(barrier, inc=1, device_id=x_left, device_id_type=MESH)

    loads = []
    for t in range(6):
        src = fs if t < 4 else cs
        lane = 128 * (t if t < 4 else t - 4)
        loads.append(
            pltpu.make_async_copy(src.at[:, :, pl.ds(lane, 128)], Q.at[t, :, pl.ds(0, NODES)], in_sem.at[t])
        )
    for t in range(6):
        src = fr if t < 4 else cr
        lane = 128 * (t if t < 4 else t - 4)
        loads.append(
            pltpu.make_async_copy(src.at[:, :, pl.ds(lane, 128)], G.at[t], in_sem.at[6 + t])
        )
    for copy in loads:
        copy.start()

    for t in range(6):
        for v in range(5):
            Q[t, v, pl.ds(NODES, ROWS - NODES), :] = jnp.full(
                (ROWS - NODES, 128), (1.0, 0.0, 0.0, 0.0, 2.5)[v], F32
            )
    for t in range(2):
        BB[t, pl.ds(180, 4), :] = jnp.zeros((4, 128), F32)
        BB[t, pl.ds(364, 20), :] = jnp.zeros((20, 128), F32)
    for t in range(4):
        PM[t, pl.ds(180, 76), :] = jnp.zeros((76, 128), F32)
        for v in range(5):
            MS[t, v, pl.ds(36, 12), :] = jnp.zeros((12, 128), F32)

    owner = own[...]
    spread = (lanes_of((16, 128)) // 8 == rows_of((16, 128))).astype(BF16)
    here = lanes_of((8, 128)) % 8 == rows_of((8, 128))

    def as_row(part):
        wide = dot_nn(part.astype(F32).astype(BF16), spread)
        return jnp.sum(jnp.where(here, wide, 0.0), axis=0, keepdims=True)

    slot_row = as_row(owner % CE)
    device_row = as_row(owner // CE).astype(jnp.int32)
    block_row = lax.rem(lax.rem(device_row, npy) + npy - py, npy)
    hits = (rows_of((16, 128)) == block_row).astype(BF16)
    earlier = (rows_of((128, 128)) < lanes_of((128, 128))).astype(BF16)
    rank = jnp.sum(hits.astype(F32) * dot_nn(hits, earlier), axis=0, keepdims=True)
    place_row = block_row.astype(F32) * most + rank
    named = (hits.astype(F32) * (slot_row + 1.0)).astype(BF16)
    turn = (rows_of((128, 128)).astype(F32) == rank).astype(BF16)
    asked = dot_nt(named, turn) - 1.0
    for d in range(npy):
        req[d] = asked[d : d + 1]
    wanted[0] = asked[0:1]
    parent = (lanes_of((128, 512)) // 32) * 8 + (lanes_of((128, 512)) % 16) // 2
    family = (parent == rows_of((128, 512))).astype(BF16)
    place_wide = dot_nn(jnp.broadcast_to(place_row, (8, 128)).astype(BF16), family)[0:1]
    SEL[...] = (rows_of((SLOTS, 512)).astype(F32) == place_wide).astype(BF16)

    pl.semaphore_wait(barrier, npy + 1)

    req_copies = [None] + [
        remote(req.at[d], wanted.at[d], req_s.at[d], req_r.at[d], up[d]) for d in range(1, npy)
    ]
    for copy in req_copies[1:]:
        copy.start()

    def x_copies(section):
        if section == 0:
            low, high = fs.at[:, pl.ds(0, 40), pl.ds(0, 128)], fs.at[:, pl.ds(176, 40), pl.ds(384, 128)]
        else:
            low, high = Q.at[0, :, pl.ds(0, 40)], Q.at[3, :, pl.ds(176, 40)]
        return [
            remote(low, hx.at[section, 0], h_s.at[section, 0], h_r.at[section, 0], x_left),
            remote(high, hx.at[section, 1], h_s.at[section, 1], h_r.at[section, 1], x_right),
        ]

    def y_copies(section):
        return [
            remote(hyo.at[section, 0], hy.at[section, 0], h_s.at[section, 2], h_r.at[section, 2], y_left),
            remote(hyo.at[section, 1], hy.at[section, 1], h_s.at[section, 3], h_r.at[section, 3], y_right),
        ]

    def y_trace(ref, t, v, j):
        return jnp.concatenate([ref[t, v, pl.ds(36 * i + 6 * j, 8), :] for i in range(6)], axis=0)

    def pack_y(section):
        residue = lanes_of((48, 128)) % 16
        for v in range(5):
            low = y_trace(Q, 0, v, 0)
            high = pltpu.roll(y_trace(Q, 0, v, 5), 113, 1)
            for t in range(1, 4):
                low = jnp.where(residue == t, pltpu.roll(y_trace(Q, t, v, 0), t, 1), low)
                high = jnp.where(residue == t, pltpu.roll(y_trace(Q, t, v, 5), 113 + t, 1), high)
            hyo[section, 0, v] = low
            hyo[section, 1, v] = high

    def volume(first, last, scale):
        def tile(t, carry):
            def chunk(c, inner):
                rows = pl.ds(pl.multiple_of(c * 24, 8), 24)
                r, m1, m2, m3, e = [Q[t, v, rows, :] for v in range(5)]
                inverse = 1.0 / r
                u1, u2, u3 = m1 * inverse, m2 * inverse, m3 * inverse
                p = pressure_of((r, m1, m2, m3, e), inverse)
                h = e + p
                for s, value in enumerate(
                    (m1 * u1 + p, m2 * u1, m3 * u1, m2 * u2 + p, m3 * u2, m3 * u3 + p, h * u1, h * u2, h * u3)
                ):
                    FX[t, s, rows, :] = value
                return inner

            lax.fori_loop(0, NODES // 24, chunk, 0)
            for v in range(5):
                for d in range(3):
                    flow = Q.at[t, 1 + d] if v == 0 else FX.at[t, 6 + d if v == 4 else PAIRS[(v - 1, d)]]
                    for spans in lines(d):
                        out = differ([flow[at, :] for at in spans], scale)
                        for at, value in zip(spans, out):
                            if d == 0:
                                R[t, v, at, :] = value
                            else:
                                R[t, v, at, :] = R[t, v, at, :] + value
            return carry

        lax.fori_loop(first, last, tile, 0)

    def differ(f, scale):
        even = [f[j] + f[5 - j] for j in range(3)]
        odd = [f[j] - f[5 - j] for j in range(3)]
        first, second = even[0] - even[2], even[1] - even[2]
        out = [None] * 6
        for i in range(3):
            a = float(scale * even_table[i, 0]) * first + float(scale * even_table[i, 1]) * second
            b = float(scale * odd_table[i, 0]) * odd[0] + float(scale * odd_table[i, 1]) * odd[1]
            b = b + float(scale * odd_table[i, 2]) * odd[2]
            out[i], out[5 - i] = b + a, b - a
        return out

    def bottom(t):
        return [Q[t, v, pl.ds(0, 36, stride=6), :] for v in range(5)]

    def coarse_own():
        for t in (4, 5):
            parts = flux(bottom(t), 2)[0]
            for v in range(5):
                at = pl.ds(0, 36, stride=6)
                R[t, v, at, :] = R[t, v, at, :] - lift * parts[v]

    def x_faces(section):
        lane = lanes_of((36, 128))

        def minus(t):
            if t == 4:
                return [hx[section, 0, v, pl.ds(0, 36), :] for v in range(5)]
            return [Q[t, v, pl.ds(0, 36), :] for v in range(5)]

        def plus(t):
            if t < 0:
                return [hx[section, 1, v, pl.ds(4, 36), :] for v in range(5)]
            return [Q[t, v, pl.ds(180, 36), :] for v in range(5)]

        before = [pltpu.roll(x, 16, 1) for x in plus(-1)]
        held = None
        for t in range(5):
            right = minus(t)
            if t < 4:
                mine = [pltpu.roll(x, 16, 1) for x in plus(t)]
                left = [jnp.where(lane < 16, b, m) for b, m in zip(before, mine)]
                before = mine
            else:
                left = before
            lf, ls = flux_speed(left, 0)
            rf, rs = flux_speed(right, 0)
            low = blend(left, lf, ls, right, rf, rs)
            if t < 4:
                for v in range(5):
                    at = pl.ds(0, 36)
                    R[t, v, at, :] = R[t, v, at, :] + lift2 * (low[v] - rf[v])
            turned = [pltpu.roll(x, 112, 1) for x in low]
            if t > 0:
                own_flux = flux(plus(t - 1), 0)[0]
                for v in range(5):
                    high = jnp.where(lane >= 112, turned[v], held[v])
                    at = pl.ds(180, 36)
                    R[t - 1, v, at, :] = R[t - 1, v, at, :] + lift2 * (own_flux[v] - high)
            held = turned

    def y_faces(section):
        residue = lanes_of((48, 128)) % 16
        edge_left = [hyo[section, 1, v] for v in range(5)]
        edge_right = [hy[section, 0, v] for v in range(5)]
        lf, ls = flux_speed(edge_left, 1)
        rf, rs = flux_speed(edge_right, 1)
        edge = blend(edge_left, lf, ls, edge_right, rf, rs)
        for t in range(4):
            right = [y_trace(Q, t, v, 0) for v in range(5)]
            upper = [y_trace(Q, t, v, 5) for v in range(5)]
            left = [
                jnp.where(
                    residue == 0,
                    pltpu.roll(hy[section, 1, v], (128 - t) % 128, 1),
                    pltpu.roll(upper[v], 1, 1),
                )
                for v in range(5)
            ]
            lf, ls = flux_speed(left, 1)
            rf, rs = flux_speed(right, 1)
            low = blend(left, lf, ls, right, rf, rs)
            own_flux = flux(upper, 1)[0]
            for v in range(5):
                high = jnp.where(residue == 15, pltpu.roll(edge[v], 15 - t, 1), pltpu.roll(low[v], 127, 1))
                down_term = lift2 * (low[v] - rf[v])
                up_term = lift2 * (own_flux[v] - high)
                for i in range(6):
                    at = pl.ds(36 * i, 6)
                    R[t, v, at, :] = R[t, v, at, :] + down_term[8 * i : 8 * i + 6]
                    at = pl.ds(36 * i + 30, 6)
                    R[t, v, at, :] = R[t, v, at, :] + up_term[8 * i : 8 * i + 6]

    def ground():
        for t in range(4):
            q = bottom(t)
            parts, speed = flux_speed(q, 2)
            change = [parts[0], parts[1], parts[2], speed * q[3], parts[4]]
            for v in range(5):
                at = pl.ds(0, 36, stride=6)
                R[t, v, at, :] = R[t, v, at, :] - lift2 * change[v]

    def pick(wide, t):
        lane = lanes_of((36, 128))
        odd_a = (lane // 16) % 2 == 1
        odd_b = lane % 2 == 1
        part = [wide[40 * g : 40 * g + 36, 128 * t : 128 * t + 128] for g in range(4)]
        return jnp.where(odd_a, jnp.where(odd_b, part[3], part[2]), jnp.where(odd_b, part[1], part[0]))

    def mortar(section):
        lifted = []
        for v in range(5):
            rows = pl.ds(36 * v, 48)
            coarse_trace = jnp.concatenate([S[0, rows, :], S[1, rows, :]], axis=1)
            both = jnp.concatenate(split(coarse_trace), axis=0)
            wide = dot_nn(both, SEL[...]).astype(BF16)
            stack = jnp.concatenate([wide, wide[:48]], axis=0)
            lifted.append(dot_nn(pst[...], stack))
        for t in range(4):
            left = [Q[t, v, pl.ds(5, 36, stride=6), :] for v in range(5)]
            right = [pick(lifted[v], t) for v in range(5)]
            lf, ls = flux_speed(left, 2)
            rf, rs = flux_speed(right, 2)
            upper = blend(left, lf, ls, right, rf, rs)
            for v in range(5):
                TOPC[t, v, pl.ds(0, 36), :] = lift2 * (lf[v] - upper[v])
                MS[t, v, pl.ds(0, 36), :] = upper[v]
        for v in range(5):
            whole = jnp.concatenate([MS[t, v] for t in range(4)], axis=1)
            high, low = split(whole)
            wide = dot_nn(qst[...], jnp.concatenate([high, low, high], axis=0))
            for t in range(4):
                PM[t, pl.ds(36 * v, 36), :] = pick(wide, t)
        high, low = split(jnp.concatenate([PM[t] for t in range(4)], axis=1))
        sent = dot_nt(SEL[...], high) + dot_nt(SEL[...], low)
        sent = sent.reshape(npy, most, 256)
        fout[section] = sent
        fin[section, 0] = sent[0]
        for copy in f_copies[section][1:]:
            copy.start()
        if section == 0:
            for copy in rest_copies[1:]:
                copy.wait_recv()
            received = incb[...].reshape(SLOTS, 128).T
            S[0, pl.ds(256, 128), :] = received[:, :128]
            S[1, pl.ds(256, 128), :] = received[:, 128:]
            face = dot_nt(high, SEL[...]) + dot_nt(low, SEL[...])
            for t in range(2):
                rows = pl.ds(0, 184)
                S[t, rows, :] = S[t, rows, :] + section_coefs[0][1] * (
                    S[t, pl.ds(184, 184), :] + lift * face[:184, 128 * t : 128 * t + 128]
                )

    f_copies = [
        [None]
        + [
            remote(fout.at[s, d], fin.at[s, d], f_s.at[s, d], f_r.at[s, d], up[d])
            for d in range(1, npy)
        ]
        for s in range(2)
    ]

    def fine_update(section):
        decay, step = section_coefs[section]
        for t in range(4):
            for v in range(5):
                at = pl.ds(5, 36, stride=6)
                R[t, v, at, :] = R[t, v, at, :] + TOPC[t, v, pl.ds(0, 36), :]

        def one(v, carry):
            for t in range(4):
                new = decay * G[t, v] + R[t, v, pl.ds(0, NODES), :]
                G[t, v] = new
                rows = pl.ds(0, NODES)
                Q[t, v, rows, :] = Q[t, v, rows, :] + step * new
            return carry

        lax.fori_loop(0, 5, one, 0)

    count = cnt[0]

    def coarse_update(section):
        decay, step = section_coefs[section]
        for copy in f_copies[section][1:]:
            copy.wait_recv()
        arrived = fin[section].reshape(SLOTS, 256).T
        high, low = split(arrived[:184])
        face = dot_nn(high, W[...]) + dot_nn(low, W[...])
        for t in range(2):
            for v in range(5):
                at = pl.ds(0, 36, stride=6)
                R[4 + t, v, at, :] = (
                    R[4 + t, v, at, :] + lift * face[36 * v : 36 * v + 36, 128 * t : 128 * t + 128]
                )

        def one(v, carry):
            for t in range(2):
                live = lanes_of((NODES, 128)) + 128 * t < count
                rows = pl.ds(0, NODES)
                old = G[4 + t, v]
                new = jnp.where(live, decay * old + R[4 + t, v, rows, :], old)
                G[4 + t, v] = new
                state = Q[4 + t, v, rows, :]
                Q[4 + t, v, rows, :] = jnp.where(live, state + step * new, state)
            return carry

        lax.fori_loop(0, 5, one, 0)

    x_sends = [x_copies(0), x_copies(1)]
    y_sends = [y_copies(0), y_copies(1)]
    for copy in x_sends[0]:
        copy.start()
    for t in range(4):
        loads[t].wait()
    pack_y(0)
    for copy in y_sends[0]:
        copy.start()
    for t in (4, 5, 10, 11):
        loads[t].wait()
    volume(4, 6, -dt)
    coarse_own()
    at = pl.ds(0, 36, stride=6)
    for t in range(2):
        for v in range(5):
            BB[t, pl.ds(36 * v, 36), :] = Q[4 + t, v, at, :]
            BB[t, pl.ds(184 + 36 * v, 36), :] = section_coefs[0][0] * G[4 + t, v, at, :] + R[4 + t, v, at, :]
    for copy in req_copies[1:]:
        copy.wait_recv()
    row = jnp.concatenate([jnp.broadcast_to(wanted[d], (most, 128)) for d in range(npy)], axis=0)
    mine = lanes_of((SLOTS, 128)) == rows_of((SLOTS, 128)) % most
    want = jnp.sum(jnp.where(mine, row, 0.0), axis=1, keepdims=True)
    number = lanes_of((SLOTS, 128)).astype(F32)
    W[...] = jnp.concatenate([want == number, want == number + 128.0], axis=1).astype(BF16)
    high, low = split(jnp.concatenate([BB[0], BB[1]], axis=1))
    reply = (dot_nt(W[...], high) + dot_nt(W[...], low)).reshape(npy, most, 384)
    rep[...] = reply[:, :, :256]
    rest[...] = reply[:, :, 256:]
    inc[0] = reply[0, :, :256]
    incb[0] = reply[0, :, 256:]
    rep_copies = [None] + [
        remote(rep.at[d], inc.at[d], rep_s.at[0, d], rep_r.at[0, d], down[d]) for d in range(1, npy)
    ]
    rest_copies = [None] + [
        remote(rest.at[d], incb.at[d], rep_s.at[1, d], rep_r.at[1, d], down[d]) for d in range(1, npy)
    ]
    for copy in rep_copies[1:] + rest_copies[1:]:
        copy.start()
    volume(0, 4, -2.0 * dt)
    ground()
    for copy in x_sends[0] + y_sends[0]:
        copy.wait_recv()
    x_faces(0)
    y_faces(0)
    for copy in rep_copies[1:]:
        copy.wait_recv()
    received = inc[...].reshape(SLOTS, 256).T
    S[0, pl.ds(0, 256), :] = received[:, :128]
    S[1, pl.ds(0, 256), :] = received[:, 128:]
    mortar(0)
    for t in range(6, 10):
        loads[t].wait()
    fine_update(0)

    pack_y(1)
    for copy in x_sends[1] + y_sends[1]:
        copy.start()
    mortar(1)
    coarse_update(0)
    volume(4, 6, -dt)
    coarse_own()
    volume(0, 4, -2.0 * dt)
    ground()
    for copy in x_sends[1] + y_sends[1]:
        copy.wait_recv()
    x_faces(1)
    y_faces(1)
    for copy in x_sends[1]:
        copy.wait_send()
    fine_update(1)
    stores = []
    for t in range(6):
        lane = 128 * (t if t < 4 else t - 4)
        stores.append(
            pltpu.make_async_copy(
                Q.at[t, :, pl.ds(0, NODES)], (ofs if t < 4 else ocs).at[:, :, pl.ds(lane, 128)], out_sem.at[t]
            )
        )
        stores.append(
            pltpu.make_async_copy(
                G.at[t], (ofr if t < 4 else ocr).at[:, :, pl.ds(lane, 128)], out_sem.at[6 + t]
            )
        )
    for copy in stores[:8]:
        copy.start()
    coarse_update(1)
    for copy in stores[8:]:
        copy.start()
    for copy in req_copies[1:] + rep_copies[1:] + rest_copies[1:] + f_copies[0][1:] + f_copies[1][1:]:
        copy.wait_send()
    for copy in x_sends[0] + y_sends[0] + y_sends[1]:
        copy.wait_send()
    for copy in stores:
        copy.wait()


def body(shape, fine_state, fine_register, coarse_state, coarse_register, coarse_owner, coarse_count):
    npx, npy = shape
    most = SLOTS // npy
    even_table, odd_table, pst, qst, lifting = make_tables()
    anyspace = pl.BlockSpec(memory_space=pl.ANY)
    vmem = pl.BlockSpec(memory_space=pltpu.VMEM)
    dma = pltpu.SemaphoreType.DMA
    fine = jax.ShapeDtypeStruct((5, NODES, EX * EY), F32)
    coarse = jax.ShapeDtypeStruct((5, NODES, CE), F32)
    return pl.pallas_call(
        functools.partial(kernel, shape, lifting, even_table, odd_table),
        out_shape=(fine, fine, coarse, coarse),
        in_specs=[anyspace] * 4 + [vmem, pl.BlockSpec(memory_space=pltpu.SMEM)] + [vmem] * 2,
        out_specs=(anyspace,) * 4,
        scratch_shapes=[
            pltpu.VMEM((6, 5, ROWS, 128), F32),
            pltpu.VMEM((6, 5, NODES, 128), F32),
            pltpu.VMEM((6, 5, ROWS, 128), F32),
            pltpu.VMEM((6, 9, NODES, 128), F32),
            pltpu.VMEM((2, 384, 128), F32),
            pltpu.VMEM((2, 384, 128), F32),
            pltpu.VMEM((SLOTS, CE), BF16),
            pltpu.VMEM((SLOTS, 512), BF16),
            pltpu.VMEM((4, 5, 48, 128), F32),
            pltpu.VMEM((4, 256, 128), F32),
            pltpu.VMEM((4, 5, 40, 128), F32),
            pltpu.VMEM((npy, 1, 128), F32),
            pltpu.VMEM((npy, 1, 128), F32),
            pltpu.VMEM((npy, most, 256), F32),
            pltpu.VMEM((npy, most, 256), F32),
            pltpu.VMEM((npy, most, 128), F32),
            pltpu.VMEM((npy, most, 128), F32),
            pltpu.VMEM((2, npy, most, 256), F32),
            pltpu.VMEM((2, npy, most, 256), F32),
            pltpu.VMEM((2, 2, 5, 40, 128), F32),
            pltpu.VMEM((2, 2, 5, 48, 128), F32),
            pltpu.VMEM((2, 2, 5, 48, 128), F32),
            dma((12,)),
            dma((12,)),
            dma((npy,)),
            dma((npy,)),
            dma((2, npy)),
            dma((2, npy)),
            dma((2, npy)),
            dma((2, npy)),
            dma((2, 4)),
            dma((2, 4)),
        ],
        compiler_params=pltpu.CompilerParams(
            collective_id=0, has_side_effects=True, vmem_limit_bytes=56 << 20
        ),
    )(
        fine_state, fine_register, coarse_state, coarse_register, coarse_owner.T, coarse_count,
        jnp.asarray(pst), jnp.asarray(qst),
    )


def solution(mesh):
    whole = P(None, None, ("px", "py"))
    return jax.shard_map(
        functools.partial(body, (mesh.shape["px"], mesh.shape["py"])),
        mesh=mesh,
        in_specs=(whole, whole, whole, whole, P("px", "py"), P(("px", "py"))),
        out_specs=(whole,) * 4,
        check_vma=False,
    )
```

```python
import functools
import math

import jax
import jax.numpy as jnp
import numpy as np
from jax import lax
from jax.experimental import pallas as pl
from jax.experimental.pallas import tpu as pltpu
from jax.sharding import PartitionSpec as P

NP = 6
NODES = 216
ROWS = 224
EX = 32
EY = 16
CE = 256
SLOTS = 256

time_step = 0.01
section_coefs = ((-0.4178904745, 0.3792103129), (-1.192151694643, 0.8229550293869))
MESH = pl.DeviceIdType.MESH
F32 = jnp.float32
BF16 = jnp.bfloat16


def legendre_columns(nodes, points):
    columns = [np.ones(points), nodes]
    for degree in range(2, points):
        columns.append(
            ((2 * degree - 1) * nodes * columns[-1] - (degree - 1) * columns[-2]) / degree
        )
    return columns


def node_tables(points):
    order = points - 1
    nodes = np.array([-math.cos(math.pi * index / order) for index in range(points)])
    for sweep in range(60):
        columns = legendre_columns(nodes, points)
        nodes = nodes - (nodes * columns[order] - columns[order - 1]) / (points * columns[order])
    legendre = legendre_columns(nodes, points)[order]
    weights = 2.0 / (order * points * legendre**2)
    same = np.arange(points)[:, None] == np.arange(points)[None, :]
    spread = nodes[:, None] - nodes[None, :] + np.where(same, 1.0, 0.0)
    barycentric = 1.0 / np.prod(spread, axis=1)
    derivative = np.where(same, 0.0, barycentric[None, :] / barycentric[:, None] / spread)
    derivative = derivative - np.where(same, np.sum(derivative, axis=1)[:, None], 0.0)
    halves = []
    for side in (-1.0, 1.0):
        target = 0.5 * (nodes + side)
        table = np.ones((points, points))
        for column in range(points):
            for other in range(points):
                if other != column:
                    table[:, column] *= (target - nodes[other]) / (nodes[column] - nodes[other])
        halves.append(table)
    to_fine = np.stack(halves)
    to_coarse = 0.5 * to_fine.transpose(0, 2, 1) * weights[None, None, :] / weights[None, :, None]
    f = np.float32
    return derivative, to_fine.astype(f), to_coarse.astype(f), float(1.0 / weights[0])


def halves_of(table):
    high = np.asarray(table, np.float32).astype(BF16)
    low = (np.asarray(table, np.float32) - high.astype(np.float32)).astype(BF16)
    return high, low


def make_tables():
    derivative, to_fine, to_coarse, lifting = node_tables(NP)
    even_table = 0.5 * (derivative[:3, :3] + derivative[:3, 5:2:-1])
    odd_table = 0.5 * (derivative[:3, :3] - derivative[:3, 5:2:-1])
    stacks = []
    for table in (to_fine, to_coarse):
        full = np.zeros((160, 48), np.float32)
        for a in range(2):
            for b in range(2):
                r = (2 * a + b) * 40
                full[r : r + 36, :36] = np.kron(table[a], table[b])
        th, tl = halves_of(full)
        stacks.append(np.concatenate([th, th, tl], axis=1))
    return even_table, odd_table, stacks[0], stacks[1], lifting


PAIRS = {(0, 0): 0, (0, 1): 1, (0, 2): 2, (1, 0): 1, (1, 1): 3, (1, 2): 4, (2, 0): 2, (2, 1): 4, (2, 2): 5}


def lines(d):
    sizes = (8, 8, 8, 8, 4)
    if d == 0:
        return [[pl.ds(36 * i + 8 * c, sizes[c]) for i in range(6)] for c in range(5)]
    if d == 1:
        return [[pl.ds(36 * i + 6 * j, 6) for j in range(6)] for i in range(6)]
    return [[pl.ds(48 * c + k, sizes[c], stride=6) for k in range(6)] for c in range(5)]


def split(x):
    high = x.astype(BF16)
    low = (x - high.astype(F32)).astype(BF16)
    return high, low


def dot_nn(a, b):
    return lax.dot_general(a, b, (((1,), (0,)), ((), ())), preferred_element_type=F32)


def dot_nt(a, b):
    return lax.dot_general(a, b, (((1,), (1,)), ((), ())), preferred_element_type=F32)


def pressure_of(q, inverse):
    return 0.4 * (q[4] - 0.5 * (q[1] * q[1] + q[2] * q[2] + q[3] * q[3]) * inverse)


def flux(q, d):
    inverse = 1.0 / q[0]
    velocity = q[1 + d] * inverse
    pressure = pressure_of(q, inverse)
    parts = [q[1 + d], q[1] * velocity, q[2] * velocity, q[3] * velocity, (q[4] + pressure) * velocity]
    parts[1 + d] = parts[1 + d] + pressure
    return parts, velocity, pressure, inverse


def flux_speed(q, d):
    parts, velocity, pressure, inverse = flux(q, d)
    return parts, jnp.abs(velocity) + jnp.sqrt(1.4 * pressure * inverse)


def blend(left, left_flux, left_speed, right, right_flux, right_speed):
    fastest = 0.5 * jnp.maximum(left_speed, right_speed)
    return [
        0.5 * (lf + rf) - fastest * (r - l)
        for l, lf, r, rf in zip(left, left_flux, right, right_flux)
    ]


def lanes_of(shape):
    return lax.broadcasted_iota(jnp.int32, shape, len(shape) - 1)


def rows_of(shape):
    return lax.broadcasted_iota(jnp.int32, shape, len(shape) - 2)


def kernel(
    shape, lifting, even_table, odd_table,
    fs, fr, cs, cr, own, cnt, pst, qst,
    Q, G, R, FX, BB, S, W, SEL, MS, PM, TOPC,
    req, wanted, rep, inc, rest, incb, fout, fin, hx, hyo, hy,
    in_sem, req_s, req_r, rep_s, rep_r, f_s, f_r, h_s, h_r,
):
    npx, npy = shape
    most = SLOTS // npy
    px = lax.axis_index("px")
    py = lax.axis_index("py")
    up = [(px, lax.rem(py + d, npy)) for d in range(npy)]
    down = [(px, lax.rem(py + npy - d, npy)) for d in range(npy)]
    x_right, x_left = (lax.rem(px + 1, npx), py), (lax.rem(px + npx - 1, npx), py)
    y_right, y_left = up[1], down[1]
    dt = time_step
    lift = dt * lifting
    lift2 = 2.0 * lift

    def remote(src, dst, ss, rs, dev):
        return pltpu.make_async_remote_copy(
            src_ref=src, dst_ref=dst, send_sem=ss, recv_sem=rs, device_id=dev, device_id_type=MESH
        )

    barrier = pltpu.get_barrier_semaphore()
    for d in range(1, npy):
        pl.semaphore_signal(barrier, inc=1, device_id=up[d], device_id_type=MESH)
    pl.semaphore_signal(barrier, inc=1, device_id=x_right, device_id_type=MESH)
    pl.semaphore_signal(barrier, inc=1, device_id=x_left, device_id_type=MESH)

    loads = []
    for t in range(6):
        src = fs if t < 4 else cs
        lane = 128 * (t if t < 4 else t - 4)
        loads.append(
            pltpu.make_async_copy(src.at[:, :, pl.ds(lane, 128)], Q.at[t, :, pl.ds(0, NODES)], in_sem.at[t])
        )
    for t in range(6):
        src = fr if t < 4 else cr
        lane = 128 * (t if t < 4 else t - 4)
        loads.append(
            pltpu.make_async_copy(src.at[:, :, pl.ds(lane, 128)], G.at[t], in_sem.at[6 + t])
        )
    for copy in loads:
        copy.start()

    for t in range(6):
        for v in range(5):
            Q[t, v, pl.ds(NODES, ROWS - NODES), :] = jnp.full(
                (ROWS - NODES, 128), (1.0, 0.0, 0.0, 0.0, 2.5)[v], F32
            )
    for t in range(2):
        BB[t, pl.ds(180, 4), :] = jnp.zeros((4, 128), F32)
        BB[t, pl.ds(364, 20), :] = jnp.zeros((20, 128), F32)
    for t in range(4):
        PM[t, pl.ds(180, 76), :] = jnp.zeros((76, 128), F32)
        for v in range(5):
            MS[t, v, pl.ds(36, 12), :] = jnp.zeros((12, 128), F32)

    owner = own[...]
    spread = (lanes_of((16, 128)) // 8 == rows_of((16, 128))).astype(BF16)
    here = lanes_of((8, 128)) % 8 == rows_of((8, 128))

    def as_row(part):
        wide = dot_nn(part.astype(F32).astype(BF16), spread)
        return jnp.sum(jnp.where(here, wide, 0.0), axis=0, keepdims=True)

    slot_row = as_row(owner % CE)
    device_row = as_row(owner // CE).astype(jnp.int32)
    block_row = lax.rem(lax.rem(device_row, npy) + npy - py, npy)
    hits = (rows_of((16, 128)) == block_row).astype(BF16)
    earlier = (rows_of((128, 128)) < lanes_of((128, 128))).astype(BF16)
    rank = jnp.sum(hits.astype(F32) * dot_nn(hits, earlier), axis=0, keepdims=True)
    place_row = block_row.astype(F32) * most + rank
    named = (hits.astype(F32) * (slot_row + 1.0)).astype(BF16)
    turn = (rows_of((128, 128)).astype(F32) == rank).astype(BF16)
    asked = dot_nt(named, turn) - 1.0
    for d in range(npy):
        req[d] = asked[d : d + 1]
    wanted[0] = asked[0:1]
    parent = (lanes_of((128, 512)) // 32) * 8 + (lanes_of((128, 512)) % 16) // 2
    family = (parent == rows_of((128, 512))).astype(BF16)
    place_wide = dot_nn(jnp.broadcast_to(place_row, (8, 128)).astype(BF16), family)[0:1]
    SEL[...] = (rows_of((SLOTS, 512)).astype(F32) == place_wide).astype(BF16)

    pl.semaphore_wait(barrier, npy + 1)

    req_copies = [None] + [
        remote(req.at[d], wanted.at[d], req_s.at[d], req_r.at[d], up[d]) for d in range(1, npy)
    ]
    for copy in req_copies[1:]:
        copy.start()

    def x_copies(section):
        if section == 0:
            low, high = fs.at[:, pl.ds(0, 40), pl.ds(0, 128)], fs.at[:, pl.ds(176, 40), pl.ds(384, 128)]
        else:
            low, high = Q.at[0, :, pl.ds(0, 40)], Q.at[3, :, pl.ds(176, 40)]
        return [
            remote(low, hx.at[section, 0], h_s.at[section, 0], h_r.at[section, 0], x_left),
            remote(high, hx.at[section, 1], h_s.at[section, 1], h_r.at[section, 1], x_right),
        ]

    def y_copies(section):
        return [
            remote(hyo.at[section, 0], hy.at[section, 0], h_s.at[section, 2], h_r.at[section, 2], y_left),
            remote(hyo.at[section, 1], hy.at[section, 1], h_s.at[section, 3], h_r.at[section, 3], y_right),
        ]

    def y_trace(ref, t, v, j):
        return jnp.concatenate([ref[t, v, pl.ds(36 * i + 6 * j, 8), :] for i in range(6)], axis=0)

    def pack_y(section):
        residue = lanes_of((48, 128)) % 16
        for v in range(5):
            low = y_trace(Q, 0, v, 0)
            high = pltpu.roll(y_trace(Q, 0, v, 5), 113, 1)
            for t in range(1, 4):
                low = jnp.where(residue == t, pltpu.roll(y_trace(Q, t, v, 0), t, 1), low)
                high = jnp.where(residue == t, pltpu.roll(y_trace(Q, t, v, 5), 113 + t, 1), high)
            hyo[section, 0, v] = low
            hyo[section, 1, v] = high

    def volume(first, last, scale):
        def tile(t, carry):
            def chunk(c, inner):
                rows = pl.ds(pl.multiple_of(c * 24, 8), 24)
                r, m1, m2, m3, e = [Q[t, v, rows, :] for v in range(5)]
                inverse = 1.0 / r
                u1, u2, u3 = m1 * inverse, m2 * inverse, m3 * inverse
                p = pressure_of((r, m1, m2, m3, e), inverse)
                h = e + p
                for s, value in enumerate(
                    (m1 * u1 + p, m2 * u1, m3 * u1, m2 * u2 + p, m3 * u2, m3 * u3 + p, h * u1, h * u2, h * u3)
                ):
                    FX[t, s, rows, :] = value
                return inner

            lax.fori_loop(0, NODES // 24, chunk, 0)
            for v in range(5):
                for d in range(3):
                    flow = Q.at[t, 1 + d] if v == 0 else FX.at[t, 6 + d if v == 4 else PAIRS[(v - 1, d)]]
                    for spans in lines(d):
                        out = differ([flow[at, :] for at in spans], scale)
                        for at, value in zip(spans, out):
                            if d == 0:
                                R[t, v, at, :] = value
                            else:
                                R[t, v, at, :] = R[t, v, at, :] + value
            return carry

        lax.fori_loop(first, last, tile, 0)

    def differ(f, scale):
        even = [f[j] + f[5 - j] for j in range(3)]
        odd = [f[j] - f[5 - j] for j in range(3)]
        first, second = even[0] - even[2], even[1] - even[2]
        out = [None] * 6
        for i in range(3):
            a = float(scale * even_table[i, 0]) * first + float(scale * even_table[i, 1]) * second
            b = float(scale * odd_table[i, 0]) * odd[0] + float(scale * odd_table[i, 1]) * odd[1]
            b = b + float(scale * odd_table[i, 2]) * odd[2]
            out[i], out[5 - i] = b + a, b - a
        return out

    def bottom(t):
        return [Q[t, v, pl.ds(0, 36, stride=6), :] for v in range(5)]

    def coarse_own():
        for t in (4, 5):
            parts = flux(bottom(t), 2)[0]
            for v in range(5):
                at = pl.ds(0, 36, stride=6)
                R[t, v, at, :] = R[t, v, at, :] - lift * parts[v]

    def x_faces(section):
        lane = lanes_of((36, 128))

        def minus(t):
            if t == 4:
                return [hx[section, 0, v, pl.ds(0, 36), :] for v in range(5)]
            return [Q[t, v, pl.ds(0, 36), :] for v in range(5)]

        def plus(t):
            if t < 0:
                return [hx[section, 1, v, pl.ds(4, 36), :] for v in range(5)]
            return [Q[t, v, pl.ds(180, 36), :] for v in range(5)]

        before = [pltpu.roll(x, 16, 1) for x in plus(-1)]
        held = None
        for t in range(5):
            right = minus(t)
            if t < 4:
                mine = [pltpu.roll(x, 16, 1) for x in plus(t)]
                left = [jnp.where(lane < 16, b, m) for b, m in zip(before, mine)]
                before = mine
            else:
                left = before
            lf, ls = flux_speed(left, 0)
            rf, rs = flux_speed(right, 0)
            low = blend(left, lf, ls, right, rf, rs)
            if t < 4:
                for v in range(5):
                    at = pl.ds(0, 36)
                    R[t, v, at, :] = R[t, v, at, :] + lift2 * (low[v] - rf[v])
            turned = [pltpu.roll(x, 112, 1) for x in low]
            if t > 0:
                own_flux = flux(plus(t - 1), 0)[0]
                for v in range(5):
                    high = jnp.where(lane >= 112, turned[v], held[v])
                    at = pl.ds(180, 36)
                    R[t - 1, v, at, :] = R[t - 1, v, at, :] + lift2 * (own_flux[v] - high)
            held = turned

    def y_faces(section):
        residue = lanes_of((48, 128)) % 16
        edge_left = [hyo[section, 1, v] for v in range(5)]
        edge_right = [hy[section, 0, v] for v in range(5)]
        lf, ls = flux_speed(edge_left, 1)
        rf, rs = flux_speed(edge_right, 1)
        edge = blend(edge_left, lf, ls, edge_right, rf, rs)
        for t in range(4):
            right = [y_trace(Q, t, v, 0) for v in range(5)]
            upper = [y_trace(Q, t, v, 5) for v in range(5)]
            left = [
                jnp.where(
                    residue == 0,
                    pltpu.roll(hy[section, 1, v], (128 - t) % 128, 1),
                    pltpu.roll(upper[v], 1, 1),
                )
                for v in range(5)
            ]
            lf, ls = flux_speed(left, 1)
            rf, rs = flux_speed(right, 1)
            low = blend(left, lf, ls, right, rf, rs)
            own_flux = flux(upper, 1)[0]
            for v in range(5):
                high = jnp.where(residue == 15, pltpu.roll(edge[v], 15 - t, 1), pltpu.roll(low[v], 127, 1))
                down_term = lift2 * (low[v] - rf[v])
                up_term = lift2 * (own_flux[v] - high)
                for i in range(6):
                    at = pl.ds(36 * i, 6)
                    R[t, v, at, :] = R[t, v, at, :] + down_term[8 * i : 8 * i + 6]
                    at = pl.ds(36 * i + 30, 6)
                    R[t, v, at, :] = R[t, v, at, :] + up_term[8 * i : 8 * i + 6]

    def ground():
        for t in range(4):
            q = bottom(t)
            parts, speed = flux_speed(q, 2)
            change = [parts[0], parts[1], parts[2], speed * q[3], parts[4]]
            for v in range(5):
                at = pl.ds(0, 36, stride=6)
                R[t, v, at, :] = R[t, v, at, :] - lift2 * change[v]

    def pick(wide, t):
        lane = lanes_of((36, 128))
        odd_a = (lane // 16) % 2 == 1
        odd_b = lane % 2 == 1
        part = [wide[40 * g : 40 * g + 36, 128 * t : 128 * t + 128] for g in range(4)]
        return jnp.where(odd_a, jnp.where(odd_b, part[3], part[2]), jnp.where(odd_b, part[1], part[0]))

    def mortar(section):
        lifted = []
        for v in range(5):
            rows = pl.ds(36 * v, 48)
            coarse_trace = jnp.concatenate([S[0, rows, :], S[1, rows, :]], axis=1)
            both = jnp.concatenate(split(coarse_trace), axis=0)
            wide = dot_nn(both, SEL[...]).astype(BF16)
            stack = jnp.concatenate([wide, wide[:48]], axis=0)
            lifted.append(dot_nn(pst[...], stack))
        for t in range(4):
            left = [Q[t, v, pl.ds(5, 36, stride=6), :] for v in range(5)]
            right = [pick(lifted[v], t) for v in range(5)]
            lf, ls = flux_speed(left, 2)
            rf, rs = flux_speed(right, 2)
            upper = blend(left, lf, ls, right, rf, rs)
            for v in range(5):
                TOPC[t, v, pl.ds(0, 36), :] = lift2 * (lf[v] - upper[v])
                MS[t, v, pl.ds(0, 36), :] = upper[v]
        for v in range(5):
            whole = jnp.concatenate([MS[t, v] for t in range(4)], axis=1)
            high, low = split(whole)
            wide = dot_nn(qst[...], jnp.concatenate([high, low, high], axis=0))
            for t in range(4):
                PM[t, pl.ds(36 * v, 36), :] = pick(wide, t)
        high, low = split(jnp.concatenate([PM[t] for t in range(4)], axis=1))
        sent = dot_nt(SEL[...], high) + dot_nt(SEL[...], low)
        sent = sent.reshape(npy, most, 256)
        fout[section] = sent
        fin[section, 0] = sent[0]
        for copy in f_copies[section][1:]:
            copy.start()
        if section == 0:
            for copy in rest_copies[1:]:
                copy.wait_recv()
            received = incb[...].reshape(SLOTS, 128).T
            S[0, pl.ds(256, 128), :] = received[:, :128]
            S[1, pl.ds(256, 128), :] = received[:, 128:]
            face = dot_nt(high, SEL[...]) + dot_nt(low, SEL[...])
            for t in range(2):
                rows = pl.ds(0, 184)
                S[t, rows, :] = S[t, rows, :] + section_coefs[0][1] * (
                    S[t, pl.ds(184, 184), :] + lift * face[:184, 128 * t : 128 * t + 128]
                )

    f_copies = [
        [None]
        + [
            remote(fout.at[s, d], fin.at[s, d], f_s.at[s, d], f_r.at[s, d], up[d])
            for d in range(1, npy)
        ]
        for s in range(2)
    ]

    def fine_update(section):
        decay, step = section_coefs[section]
        for t in range(4):
            for v in range(5):
                at = pl.ds(5, 36, stride=6)
                R[t, v, at, :] = R[t, v, at, :] + TOPC[t, v, pl.ds(0, 36), :]
        if section == 1:
            return

        def one(v, carry):
            for t in range(4):
                new = decay * G[t, v] + R[t, v, pl.ds(0, NODES), :]
                G[t, v] = new
                rows = pl.ds(0, NODES)
                Q[t, v, rows, :] = Q[t, v, rows, :] + step * new
            return carry

        lax.fori_loop(0, 5, one, 0)

    count = cnt[0]

    def coarse_update(section):
        decay, step = section_coefs[section]
        for copy in f_copies[section][1:]:
            copy.wait_recv()
        arrived = fin[section].reshape(SLOTS, 256).T
        high, low = split(arrived[:184])
        face = dot_nn(high, W[...]) + dot_nn(low, W[...])
        for t in range(2):
            for v in range(5):
                at = pl.ds(0, 36, stride=6)
                R[4 + t, v, at, :] = (
                    R[4 + t, v, at, :] + lift * face[36 * v : 36 * v + 36, 128 * t : 128 * t + 128]
                )
        if section == 1:
            return

        def one(v, carry):
            for t in range(2):
                live = lanes_of((NODES, 128)) + 128 * t < count
                rows = pl.ds(0, NODES)
                old = G[4 + t, v]
                new = jnp.where(live, decay * old + R[4 + t, v, rows, :], old)
                G[4 + t, v] = new
                state = Q[4 + t, v, rows, :]
                Q[4 + t, v, rows, :] = jnp.where(live, state + step * new, state)
            return carry

        lax.fori_loop(0, 5, one, 0)

    x_sends = [x_copies(0), x_copies(1)]
    y_sends = [y_copies(0), y_copies(1)]
    for copy in x_sends[0]:
        copy.start()
    for t in range(4):
        loads[t].wait()
    pack_y(0)
    for copy in y_sends[0]:
        copy.start()
    for t in (4, 5, 10, 11):
        loads[t].wait()
    volume(4, 6, -dt)
    coarse_own()
    at = pl.ds(0, 36, stride=6)
    for t in range(2):
        for v in range(5):
            BB[t, pl.ds(36 * v, 36), :] = Q[4 + t, v, at, :]
            BB[t, pl.ds(184 + 36 * v, 36), :] = section_coefs[0][0] * G[4 + t, v, at, :] + R[4 + t, v, at, :]
    for copy in req_copies[1:]:
        copy.wait_recv()
    row = jnp.concatenate([jnp.broadcast_to(wanted[d], (most, 128)) for d in range(npy)], axis=0)
    mine = lanes_of((SLOTS, 128)) == rows_of((SLOTS, 128)) % most
    want = jnp.sum(jnp.where(mine, row, 0.0), axis=1, keepdims=True)
    number = lanes_of((SLOTS, 128)).astype(F32)
    W[...] = jnp.concatenate([want == number, want == number + 128.0], axis=1).astype(BF16)
    high, low = split(jnp.concatenate([BB[0], BB[1]], axis=1))
    reply = (dot_nt(W[...], high) + dot_nt(W[...], low)).reshape(npy, most, 384)
    rep[...] = reply[:, :, :256]
    rest[...] = reply[:, :, 256:]
    inc[0] = reply[0, :, :256]
    incb[0] = reply[0, :, 256:]
    rep_copies = [None] + [
        remote(rep.at[d], inc.at[d], rep_s.at[0, d], rep_r.at[0, d], down[d]) for d in range(1, npy)
    ]
    rest_copies = [None] + [
        remote(rest.at[d], incb.at[d], rep_s.at[1, d], rep_r.at[1, d], down[d]) for d in range(1, npy)
    ]
    for copy in rep_copies[1:] + rest_copies[1:]:
        copy.start()
    volume(0, 4, -2.0 * dt)
    ground()
    for copy in x_sends[0] + y_sends[0]:
        copy.wait_recv()
    x_faces(0)
    y_faces(0)
    for copy in rep_copies[1:]:
        copy.wait_recv()
    received = inc[...].reshape(SLOTS, 256).T
    S[0, pl.ds(0, 256), :] = received[:, :128]
    S[1, pl.ds(0, 256), :] = received[:, 128:]
    mortar(0)
    for t in range(6, 10):
        loads[t].wait()
    fine_update(0)

    pack_y(1)
    for copy in x_sends[1] + y_sends[1]:
        copy.start()
    mortar(1)
    coarse_update(0)
    volume(4, 6, -dt)
    coarse_own()
    volume(0, 4, -2.0 * dt)
    ground()
    for copy in x_sends[1] + y_sends[1]:
        copy.wait_recv()
    x_faces(1)
    y_faces(1)
    for copy in x_sends[1]:
        copy.wait_send()
    fine_update(1)
    coarse_update(1)
    for copy in req_copies[1:] + rep_copies[1:] + rest_copies[1:] + f_copies[0][1:] + f_copies[1][1:]:
        copy.wait_send()
    for copy in x_sends[0] + y_sends[0] + y_sends[1]:
        copy.wait_send()


def finish(Q, G, R, cnt, ofs, ofr, ocs, ocr, QS, GS, out_sem):
    decay, step = section_coefs[1]
    count = cnt[0]
    stores = []
    for t in range(6):
        for v in range(5):
            old = G[t, v]
            state = Q[t, v, pl.ds(0, NODES), :]
            new = decay * old + R[t, v, pl.ds(0, NODES), :]
            moved = state + step * new
            if t >= 4:
                live = lanes_of((NODES, 128)) + 128 * (t - 4) < count
                new = jnp.where(live, new, old)
                moved = jnp.where(live, moved, state)
            GS[t, v] = new
            QS[t, v] = moved
        lanes = pl.ds(128 * (t if t < 4 else t - 4), 128)
        for k, (src, dst) in enumerate(((QS, ofs if t < 4 else ocs), (GS, ofr if t < 4 else ocr))):
            copy = pltpu.make_async_copy(src.at[t], dst.at[:, :, lanes], out_sem.at[k, t])
            copy.start()
            stores.append(copy)
    for copy in stores:
        copy.wait()


def body(shape, fine_state, fine_register, coarse_state, coarse_register, coarse_owner, coarse_count):
    npx, npy = shape
    most = SLOTS // npy
    even_table, odd_table, pst, qst, lifting = make_tables()
    anyspace = pl.BlockSpec(memory_space=pltpu.HBM)
    vmem = pl.BlockSpec(memory_space=pltpu.VMEM)
    dma = pltpu.SemaphoreType.DMA
    fine = jax.ShapeDtypeStruct((5, NODES, EX * EY), F32)
    coarse = jax.ShapeDtypeStruct((5, NODES, CE), F32)
    state, register, rate = pl.pallas_call(
        functools.partial(kernel, shape, lifting, even_table, odd_table),
        out_shape=(
            pltpu.VMEM((6, 5, ROWS, 128), F32),
            pltpu.VMEM((6, 5, NODES, 128), F32),
            pltpu.VMEM((6, 5, ROWS, 128), F32),
        ),
        in_specs=[anyspace] * 4 + [vmem, pl.BlockSpec(memory_space=pltpu.SMEM)] + [vmem] * 2,
        out_specs=(vmem,) * 3,
        scratch_shapes=[
            pltpu.VMEM((6, 9, NODES, 128), F32),
            pltpu.VMEM((2, 384, 128), F32),
            pltpu.VMEM((2, 384, 128), F32),
            pltpu.VMEM((SLOTS, CE), BF16),
            pltpu.VMEM((SLOTS, 512), BF16),
            pltpu.VMEM((4, 5, 48, 128), F32),
            pltpu.VMEM((4, 256, 128), F32),
            pltpu.VMEM((4, 5, 40, 128), F32),
            pltpu.VMEM((npy, 1, 128), F32),
            pltpu.VMEM((npy, 1, 128), F32),
            pltpu.VMEM((npy, most, 256), F32),
            pltpu.VMEM((npy, most, 256), F32),
            pltpu.VMEM((npy, most, 128), F32),
            pltpu.VMEM((npy, most, 128), F32),
            pltpu.VMEM((2, npy, most, 256), F32),
            pltpu.VMEM((2, npy, most, 256), F32),
            pltpu.VMEM((2, 2, 5, 40, 128), F32),
            pltpu.VMEM((2, 2, 5, 48, 128), F32),
            pltpu.VMEM((2, 2, 5, 48, 128), F32),
            dma((12,)),
            dma((npy,)),
            dma((npy,)),
            dma((2, npy)),
            dma((2, npy)),
            dma((2, npy)),
            dma((2, npy)),
            dma((2, 4)),
            dma((2, 4)),
        ],
        compiler_params=pltpu.CompilerParams(
            collective_id=0, has_side_effects=True, vmem_limit_bytes=56700000
        ),
    )(
        fine_state, fine_register, coarse_state, coarse_register, coarse_owner.T, coarse_count,
        jnp.asarray(pst), jnp.asarray(qst),
    )
    return pl.pallas_call(
        finish,
        out_shape=(fine, fine, coarse, coarse),
        in_specs=[vmem] * 3 + [pl.BlockSpec(memory_space=pltpu.SMEM)],
        out_specs=(anyspace,) * 4,
        scratch_shapes=[
            pltpu.VMEM((6, 5, NODES, 128), F32),
            pltpu.VMEM((6, 5, NODES, 128), F32),
            dma((2, 6)),
        ],
        compiler_params=pltpu.CompilerParams(vmem_limit_bytes=24 << 20),
    )(state, register, rate, coarse_count)


def solution(mesh):
    whole = P(None, None, ("px", "py"))
    return jax.shard_map(
        functools.partial(body, (mesh.shape["px"], mesh.shape["py"])),
        mesh=mesh,
        in_specs=(whole, whole, whole, whole, P("px", "py"), P(("px", "py"))),
        out_specs=(whole,) * 4,
        check_vma=False,
    )
```
